32 devices in a mesh: inp: 16 (over z, x, core), chan: 2 (over y).
Axes of the slice: x: 2, y: 2, z: 4, core: 2. Of those that a mesh axis runs over, the one named last changes fastest.
Arguments:
- volt: bfloat16 [32, 1024, 2, 512], P('chan', 'inp'), may hold values from -16 to 16
- mask: int32 [1024], P('inp'), may hold values 0 or 1
- table: int32 [64], replicated, may hold values from 0 to 63, each once
Outputs:
- vis: bfloat16 [16, 2, 2, 4, 2, 128, 128], P('inp', None, 'chan')
- gains: float32 [2, 16, 1024], P('chan', 'inp')
The draws below stay inside these ranges and needn't reach their ends.
Inputs may be any that keep to these rules, and one draw needn't show every extreme that they name: `table`: each tile number appears once.
All inputs are finite; a program needn't handle non-finite values. No bound on the sum of `mask` on one device may be relied on, other than what follows from the above.
Results may differ from the reference program's by a relative error of at most 0.001.
Values may be sent and summed in bfloat16 or wider, within the bound.
No kernel may reach another device: no remote copies, remote signals or barrier semaphores. Data moves between devices by JAX's collectives and lax.ppermute only.
A program may use at most 64 MiB of HBM per device.

```python
import math
import jax
import jax.numpy as jnp
from jax import lax

NI = 1024
F = 512
TB = 128
RANK = 4
ITERS = 8
KPO = 4
CPG = 16
CHAN = 32
NT = 64
N_CHAN = 2


def draw_volt(key, part):
    keys = jax.random.split(jax.random.fold_in(key, 11), 7)
    system = jnp.exp(jax.random.uniform(keys[0], (CHAN, NI, 1), jnp.float32, math.log(0.4), math.log(2.5)))
    power = jnp.exp(jax.random.uniform(keys[1], (CHAN, RANK, 1, 1), jnp.float32, math.log(4.0), math.log(64.0)))
    amplitude = jnp.sqrt(power / NI)
    noise_real = jax.random.normal(keys[2], (CHAN, NI, F), jnp.float32)
    noise_imag = jax.random.normal(keys[3], (CHAN, NI, F), jnp.float32)
    phases = jax.random.uniform(keys[4], (CHAN, NI, RANK), jnp.float32, -math.pi, math.pi)
    signal_real = jax.random.normal(keys[5], (CHAN, RANK, F), jnp.float32)
    signal_imag = jax.random.normal(keys[6], (CHAN, RANK, F), jnp.float32)
    total_real = noise_real
    total_imag = noise_imag
    for k in range(RANK):
        cos_part = jnp.cos(phases[:, :, k])[:, :, None]
        sin_part = jnp.sin(phases[:, :, k])[:, :, None]
        s_real = signal_real[:, k, :][:, None, :]
        s_imag = signal_imag[:, k, :][:, None, :]
        weight_k = amplitude[:, k, 0, 0][:, None, None]
        total_real = total_real + weight_k * (s_real * cos_part - s_imag * sin_part)
        total_imag = total_imag + weight_k * (s_real * sin_part + s_imag * cos_part)
    result = jnp.stack([total_real * system, total_imag * system], axis=2)
    return jnp.clip(result, -16.0, 16.0).astype(jnp.bfloat16)


def place_ends(entries, own_key, low, high):
    extent = entries.shape
    spot = [jax.random.randint(jax.random.fold_in(own_key, axis), (), 0, extent[axis]) for axis in range(len(extent))]
    entries = entries.at[tuple(spot)].set(low)
    longest = extent.index(max(extent))
    spot[longest] = (spot[longest] + 1) % extent[longest]
    return entries.at[tuple(spot)].set(high)


def setup_inputs(seed: int = 0) -> dict:
    key_of = jax.random.split(jax.random.key(seed), 4)
    return {
        "volt": draw_volt(jax.random.fold_in(key_of[3], 71), 0),
        "mask": place_ends((jax.random.randint(key_of[1], (NI,), 0, 16) < 15).astype(jnp.int32), jax.random.fold_in(key_of[1], 1), 0, 1),
        "table": jax.random.permutation(key_of[2], NT).astype(jnp.int32),
    }


def gram_parts(v):
    flat = v.reshape(v.shape[0], -1)
    other = jnp.concatenate([v[:, 1, :], -v[:, 0, :]], axis=1)
    dims = (((1,), (1,)), ((), ()))
    real_part = lax.dot_general(flat, flat, dims, preferred_element_type=jnp.float32) / v.shape[2]
    imag_part = lax.dot_general(other, flat, dims, preferred_element_type=jnp.float32) / v.shape[2]
    return (real_part, imag_part)

def apply_gram(real_part, imag_part, q_real, q_imag):
    rank = q_real.shape[0]
    stacked = jnp.concatenate([q_real, q_imag], axis=0)
    first = jnp.einsum('kj,ij->ki', stacked, real_part, precision=lax.Precision.HIGHEST)
    second = jnp.einsum('kj,ij->ki', stacked, imag_part, precision=lax.Precision.HIGHEST)
    return (first[:rank] - second[rank:], first[rank:] + second[:rank])

def orthonormal(z_real, z_imag):
    outs_real = []
    outs_imag = []
    for k in range(z_real.shape[0]):
        w_real = z_real[k]
        w_imag = z_imag[k]
        for l in range(k):
            c_real = jnp.sum(outs_real[l] * z_real[k] + outs_imag[l] * z_imag[k])
            c_imag = jnp.sum(outs_real[l] * z_imag[k] - outs_imag[l] * z_real[k])
            w_real = w_real - (outs_real[l] * c_real - outs_imag[l] * c_imag)
            w_imag = w_imag - (outs_real[l] * c_imag + outs_imag[l] * c_real)
        scale = lax.rsqrt(jnp.sum(w_real * w_real + w_imag * w_imag) + 1e-06)
        outs_real.append(w_real * scale)
        outs_imag.append(w_imag * scale)
    return (jnp.stack(outs_real), jnp.stack(outs_imag))

def calibrate(real_part, imag_part, rank, steps):
    count = real_part.shape[0]
    places = jnp.arange(count, dtype=jnp.float32)
    orders = jnp.arange(rank, dtype=jnp.float32)
    angle = 2.0 * math.pi / count * orders[:, None] * places[None, :]
    q_real = jnp.cos(angle) / math.sqrt(count)
    q_imag = jnp.sin(angle) / math.sqrt(count)
    for step in range(steps):
        z_real, z_imag = apply_gram(real_part, imag_part, q_real, q_imag)
        q_real, q_imag = orthonormal(z_real, z_imag)
    z_real, z_imag = apply_gram(real_part, imag_part, q_real, q_imag)
    high = lax.Precision.HIGHEST
    h_real = jnp.einsum('kj,lj->kl', q_real, z_real, precision=high) + jnp.einsum('kj,lj->kl', q_imag, z_imag, precision=high)
    h_imag = jnp.einsum('kj,lj->kl', q_real, z_imag, precision=high) - jnp.einsum('kj,lj->kl', q_imag, z_real, precision=high)
    u_real = jnp.einsum('kl,ki->li', h_real, q_real, precision=high) - jnp.einsum('kl,ki->li', h_imag, q_imag, precision=high)
    u_imag = jnp.einsum('kl,ki->li', h_imag, q_real, precision=high) + jnp.einsum('kl,ki->li', h_real, q_imag, precision=high)
    diag_model = lax.optimization_barrier(jnp.sum(u_real * q_real + u_imag * q_imag, axis=0))
    floor_value = 0.1 * jnp.mean(diag_model) + 1e-06
    return lax.rsqrt(jnp.maximum(diag_model, floor_value))

def tiles_of(gain_vec, real_part, imag_part, side):
    count = real_part.shape[0]
    outer = gain_vec[:, None] * gain_vec[None, :]
    tile_real = (outer * real_part).astype(jnp.bfloat16)
    tile_imag = (outer * imag_part).astype(jnp.bfloat16)
    blocks = count // side
    both = jnp.stack([tile_real, tile_imag], axis=0).reshape(2, blocks, side, blocks, side)
    return both.transpose(1, 3, 0, 2, 4).reshape(blocks * blocks, 2, side, side)

def reference(volt, mask, table):
    index = table.reshape(N_CHAN, NT // N_CHAN)[:, :KPO].reshape(-1)

    def one_channel(volt_c):
        v = volt_c * mask.astype(jnp.bfloat16)[:, None, None]
        real_part, imag_part = gram_parts(v)
        gain_vec = calibrate(real_part, imag_part, RANK, ITERS)
        tiles = tiles_of(gain_vec, real_part, imag_part, TB)
        chosen = jnp.take(tiles, index, axis=0).reshape(N_CHAN, KPO, 2, TB, TB)
        return (chosen, gain_vec)
    chosen, gain_all = lax.map(one_channel, volt)
    vis = chosen.reshape(N_CHAN, CPG, N_CHAN, KPO, 2, TB, TB).transpose(1, 0, 2, 3, 4, 5, 6)
    gains = gain_all.reshape(N_CHAN, CPG, NI)
    return (vis, gains)
```

```python
import functools
import math

import jax
import jax.numpy as jnp
import numpy as np
from jax import lax
from jax.experimental import pallas as pl
from jax.experimental.pallas import tpu as pltpu
from jax.sharding import PartitionSpec as P

TB = 128
RANK = 4
ITERS = 8
KPO = 4
EPS = 1e-06
SPLITS = 3

VMEM = pl.BlockSpec(memory_space=pltpu.VMEM)
SMEM = pl.BlockSpec(memory_space=pltpu.SMEM)


def first_basis(count):
    turns = np.outer(np.arange(RANK), np.arange(count)) % count
    angle = 2.0 * math.pi / count * turns
    both = np.concatenate([np.cos(angle), np.sin(angle)], axis=0)
    return (both / math.sqrt(count)).astype(np.float32)


def pieces(x):
    parts = []
    rest = x
    for k in range(SPLITS):
        part = rest.astype(jnp.bfloat16).astype(jnp.float32)
        parts.append(part)
        rest = rest - part
    return jnp.concatenate(parts, axis=0).astype(jnp.bfloat16)


def summed(y):
    rows = y.shape[0] // SPLITS
    total = y[(SPLITS - 1) * rows :]
    for k in range(SPLITS - 2, -1, -1):
        total = total + y[k * rows : (k + 1) * rows]
    return total


def swap(x):
    return jnp.concatenate([x[RANK:], x[:RANK]], axis=0)


def gram_times(v_ref, mask, sign, q):
    frames = v_ref.shape[1] // 2
    s = summed(lax.dot_general(pieces(q), v_ref[...], (((1,), (0,)), ((), ())), preferred_element_type=jnp.float32))
    left = s[:, :frames] + sign * swap(s[:, frames:])
    right = -sign * swap(left)
    y = jnp.concatenate([left, right], axis=1)
    z = summed(lax.dot_general(pieces(y), v_ref[...], (((1,), (1,)), ((), ())), preferred_element_type=jnp.float32))
    return z * (1.0 / frames) * mask


def inner(row_real, row_imag, z, sign):
    p = jnp.sum(z * row_real, axis=1, keepdims=True)
    m = jnp.sum(z * row_imag, axis=1, keepdims=True)
    return p + sign * swap(m)


def gram_schmidt(z, sign, order):
    w = z
    q = jnp.zeros_like(z)
    for l in range(RANK):
        row_real = w[l : l + 1]
        row_imag = w[RANK + l : RANK + l + 1]
        norm = jnp.sum(row_real * row_real + row_imag * row_imag, axis=1, keepdims=True)
        scale = lax.rsqrt(norm + EPS)
        q_real = row_real * scale
        q_imag = row_imag * scale
        q = jnp.where(order == l, jnp.where(sign > 0, q_real, q_imag), q)
        if l < RANK - 1:
            c = inner(q_real, q_imag, z, sign)
            c = jnp.where(order > l, c, 0.0)
            w = w - (q_real * c - q_imag * (sign * swap(c)))
    return q


def calibrate_kernel(v_ref, mask_ref, basis_ref, gains_ref, masked_ref):
    count = v_ref.shape[0]
    mask = mask_ref[...].astype(jnp.float32)
    rows = lax.broadcasted_iota(jnp.int32, (2 * RANK, 1), 0)
    sign = jnp.where(rows < RANK, 1.0, -1.0)
    order = jnp.where(rows < RANK, rows, rows - RANK)

    def step(_, q):
        return gram_schmidt(gram_times(v_ref, mask, sign, q), sign, order)

    q = lax.fori_loop(0, ITERS, step, basis_ref[...] * mask)
    z = gram_times(v_ref, mask, sign, q)
    u = jnp.zeros_like(q)
    for k in range(RANK):
        row_real = q[k : k + 1]
        row_imag = q[RANK + k : RANK + k + 1]
        h = inner(row_real, row_imag, z, sign)
        u = u + (row_real * h - row_imag * (sign * swap(h)))
    d = jnp.sum(u * q, axis=0, keepdims=True)
    floor = 0.1 * (jnp.sum(d, axis=1, keepdims=True) / count) + EPS
    gains = lax.rsqrt(jnp.maximum(d, floor))
    gains_ref[...] = gains
    masked = gains * mask
    for k in range(count // TB):
        masked_ref[k : k + 1, :] = masked[:, k * TB : (k + 1) * TB]


def tiles_kernel(owners, slots, table_ref, me_ref, v_ref, *out_refs):
    frames = v_ref.shape[1] // 2
    blocks = v_ref.shape[0] // TB
    dims = (((1,), (1,)), ((), ()))
    for d in range(owners):
        owner = lax.rem(me_ref[0] + d, owners)
        for s in range(KPO):
            tile = table_ref[owner * slots + s]
            row = pl.multiple_of((tile // blocks) * TB, TB)
            col = pl.multiple_of(lax.rem(tile, blocks) * TB, TB)
            lhs = v_ref[pl.ds(row, TB), :]
            rhs = v_ref[pl.ds(col, TB), :]
            other = jnp.concatenate([lhs[:, frames:], -lhs[:, :frames]], axis=1)
            out_refs[d][s, 0] = lax.dot_general(lhs, rhs, dims, preferred_element_type=jnp.float32) / frames
            out_refs[d][s, 1] = lax.dot_general(other, rhs, dims, preferred_element_type=jnp.float32) / frames


def scale_kernel(owners, slots, table_ref, me_ref, *refs):
    tile_refs, gain_refs, vis_ref = refs[:owners], refs[owners : 2 * owners], refs[2 * owners]
    blocks = gain_refs[0].shape[0]
    me = me_ref[0]
    for d in range(owners):
        source = lax.rem(me + owners - d, owners)
        for s in range(KPO):
            tile = table_ref[me * slots + s]
            row = gain_refs[d][pl.ds(tile // blocks, 1), :]
            col = gain_refs[d][pl.ds(lax.rem(tile, blocks), 1), :]
            outer = jnp.transpose(jnp.broadcast_to(row, (TB, TB))) * col
            for part in range(2):
                vis_ref[source, s, part] = (outer * tile_refs[d][s, part]).astype(jnp.bfloat16)


def body(volt, mask, table):
    owners = lax.axis_size("chan")
    slots = table.shape[0] // owners
    full_mask = lax.all_gather(mask, "inp", tiled=True)
    turned = lax.all_to_all(volt, "inp", split_axis=0, concat_axis=1, tiled=True)[0]
    count, _, frames = turned.shape
    flat = turned.reshape(count, 2 * frames)
    me = lax.axis_index("chan").reshape(1)
    blocks = count // TB

    def shift(x, d):
        return lax.ppermute(x, "chan", [(j, (j + d) % owners) for j in range(owners)])

    tile_shape = jax.ShapeDtypeStruct((KPO, 2, TB, TB), jnp.float32)
    tiles = pl.pallas_call(
        functools.partial(tiles_kernel, owners, slots),
        out_shape=[tile_shape] * owners,
        in_specs=[SMEM, SMEM, VMEM],
        out_specs=[VMEM] * owners,
        name="tiles",
    )(table, me, flat)
    arrived = [tiles[0]] + [shift(tiles[d], d) for d in range(1, owners)]

    gains, masked = pl.pallas_call(
        calibrate_kernel,
        out_shape=[
            jax.ShapeDtypeStruct((1, count), jnp.float32),
            jax.ShapeDtypeStruct((blocks, TB), jnp.float32),
        ],
        in_specs=[VMEM] * 3,
        out_specs=[VMEM] * 2,
        name="calibrate",
    )(flat, full_mask.reshape(1, count), first_basis(count))
    all_gains = [masked] + [shift(masked, d) for d in range(1, owners)]

    vis = pl.pallas_call(
        functools.partial(scale_kernel, owners, slots),
        out_shape=jax.ShapeDtypeStruct((owners, KPO, 2, TB, TB), jnp.bfloat16),
        in_specs=[SMEM, SMEM] + [VMEM] * (2 * owners),
        out_specs=VMEM,
        name="scale",
    )(table, me, *arrived, *all_gains)
    return (vis[None, :, None], gains.reshape(1, 1, count))


def solution(mesh):
    placed = (P("chan", "inp", None, None), P("inp"), P())
    return jax.shard_map(
        body,
        mesh=mesh,
        in_specs=placed,
        out_specs=(P("inp", None, "chan", None, None, None, None), P("chan", "inp", None)),
        check_vma=False,
    )
```

```python
import functools
import math

import jax
import jax.numpy as jnp
import numpy as np
from jax import lax
from jax.experimental import pallas as pl
from jax.experimental.pallas import tpu as pltpu
from jax.sharding import PartitionSpec as P

TB = 128
RANK = 4
ITERS = 8
KPO = 4
EPS = 1e-06
SPLITS = 2

VMEM = pl.BlockSpec(memory_space=pltpu.VMEM)
ANY = pl.BlockSpec(memory_space=pl.ANY)
SMEM = pl.BlockSpec(memory_space=pltpu.SMEM)


def first_basis(count):
    turns = np.outer(np.arange(RANK), np.arange(count)) % count
    angle = 2.0 * math.pi / count * turns
    both = np.concatenate([np.cos(angle), np.sin(angle)], axis=0)
    return (both / math.sqrt(count)).astype(np.float32)


def pieces(x):
    parts = []
    rest = x
    for k in range(SPLITS):
        part = rest.astype(jnp.bfloat16).astype(jnp.float32)
        parts.append(part)
        rest = rest - part
    return jnp.concatenate(parts, axis=0).astype(jnp.bfloat16)


def summed(y):
    rows = y.shape[0] // SPLITS
    total = y[(SPLITS - 1) * rows :]
    for k in range(SPLITS - 2, -1, -1):
        total = total + y[k * rows : (k + 1) * rows]
    return total


def swap(x):
    return jnp.concatenate([x[RANK:], x[:RANK]], axis=0)


def gram_times(v_ref, mask, sign, q):
    frames = v_ref.shape[1] // 2
    s = summed(lax.dot_general(pieces(q), v_ref[...], (((1,), (0,)), ((), ())), preferred_element_type=jnp.float32))
    left = s[:, :frames] + sign * swap(s[:, frames:])
    right = -sign * swap(left)
    y = jnp.concatenate([left, right], axis=1)
    z = summed(lax.dot_general(pieces(y), v_ref[...], (((1,), (1,)), ((), ())), preferred_element_type=jnp.float32))
    return z * (1.0 / frames) * mask


def inner(row_real, row_imag, z, turned):
    first = jnp.sum(z * row_real + turned * row_imag, axis=1, keepdims=True)
    second = jnp.sum(z * row_imag - turned * row_real, axis=1, keepdims=True)
    return first, second


def gram_schmidt(z, sign, order):
    turned = sign * swap(z)
    w = z
    reals, imags = [], []
    for l in range(RANK):
        row_real = w[l : l + 1]
        row_imag = w[RANK + l : RANK + l + 1]
        norm = jnp.sum(row_real * row_real + row_imag * row_imag, axis=1, keepdims=True)
        scale = lax.rsqrt(norm + EPS)
        reals.append(row_real * scale)
        imags.append(row_imag * scale)
        if l < RANK - 1:
            first, second = inner(row_real, row_imag, z, turned)
            keep = jnp.where(order > l, scale * scale, 0.0)
            w = w - (row_real * (first * keep) + row_imag * (second * keep))
    return jnp.concatenate(reals + imags, axis=0)


def calibrate_kernel(v_ref, mask_ref, basis_ref, gains_ref, masked_ref):
    count = v_ref.shape[0]
    mask = mask_ref[...].astype(jnp.float32)
    rows = lax.broadcasted_iota(jnp.int32, (2 * RANK, 1), 0)
    sign = jnp.where(rows < RANK, 1.0, -1.0)
    order = jnp.where(rows < RANK, rows, rows - RANK)

    def step(_, q):
        return gram_schmidt(gram_times(v_ref, mask, sign, q), sign, order)

    q = lax.fori_loop(0, ITERS, step, basis_ref[...] * mask)
    z = gram_times(v_ref, mask, sign, q)
    turned = sign * swap(z)
    u = jnp.zeros_like(q)
    for k in range(RANK):
        row_real = q[k : k + 1]
        row_imag = q[RANK + k : RANK + k + 1]
        first, second = inner(row_real, row_imag, z, turned)
        u = u + (row_real * first + row_imag * second)
    d = jnp.sum(u * q, axis=0, keepdims=True)
    floor = 0.1 * (jnp.sum(d, axis=1, keepdims=True) / count) + EPS
    gains = lax.rsqrt(jnp.maximum(d, floor))
    gains_ref[...] = gains
    masked = gains * mask
    for k in range(count // TB):
        masked_ref[k : k + 1, :] = masked[:, k * TB : (k + 1) * TB]


def product(v_ref, tile):
    frames = v_ref.shape[1] // 2
    blocks = v_ref.shape[0] // TB
    lhs = v_ref[pl.ds(pl.multiple_of((tile // blocks) * TB, TB), TB), :]
    rhs = v_ref[pl.ds(pl.multiple_of(lax.rem(tile, blocks) * TB, TB), TB), :]
    other = jnp.concatenate([lhs[:, frames:], -lhs[:, :frames]], axis=1)
    both = jnp.concatenate([lhs, other], axis=0)
    dims = (((1,), (1,)), ((), ()))
    return lax.dot_general(both, rhs, dims, preferred_element_type=jnp.float32) * (1.0 / frames)


def outer(gains_ref, tile):
    blocks = gains_ref.shape[0]
    row = gains_ref[pl.ds(tile // blocks, 1), :]
    col = gains_ref[pl.ds(lax.rem(tile, blocks), 1), :]
    return jnp.transpose(jnp.broadcast_to(row, (TB, TB))) * col


def sent_kernel(owners, slots, table_ref, me_ref, v_ref, *out_refs):
    for d in range(1, owners):
        owner = lax.rem(me_ref[0] + d, owners)
        for s in range(KPO):
            both = product(v_ref, table_ref[owner * slots + s])
            out_refs[d - 1][s, 0] = both[:TB]
            out_refs[d - 1][s, 1] = both[TB:]


def own_kernel(slots, table_ref, me_ref, v_ref, gains_ref, vis_ref, held, sem):
    me = me_ref[0]
    for s in range(KPO):
        tile = table_ref[me * slots + s]
        both = product(v_ref, tile)
        scale = outer(gains_ref, tile)
        held[s, 0] = (scale * both[:TB]).astype(jnp.bfloat16)
        held[s, 1] = (scale * both[TB:]).astype(jnp.bfloat16)
    copy = pltpu.make_async_copy(held, vis_ref.at[me], sem)
    copy.start()
    copy.wait()


def others_kernel(owners, slots, table_ref, me_ref, *refs):
    tile_refs, gain_refs = refs[: owners - 1], refs[owners - 1 : 2 * owners - 2]
    vis_ref, held, sem = refs[-3:]
    me = me_ref[0]
    copies = []
    for d in range(1, owners):
        for s in range(KPO):
            scale = outer(gain_refs[d - 1], table_ref[me * slots + s])
            for part in range(2):
                held[d - 1, s, part] = (scale * tile_refs[d - 1][s, part]).astype(jnp.bfloat16)
        source = lax.rem(me + owners - d, owners)
        copies.append(pltpu.make_async_copy(held.at[d - 1], vis_ref.at[source], sem.at[d - 1]))
        copies[-1].start()
    for copy in copies:
        copy.wait()


def gather_mask(mask):
    parts = lax.axis_size("inp")
    size = mask.shape[0]
    whole = jnp.zeros((1, parts * size), mask.dtype)
    whole = lax.dynamic_update_slice(whole, mask.reshape(1, size), (0, lax.axis_index("inp") * size))
    if parts & (parts - 1):
        return lax.psum(whole, "inp")
    step = 1
    while step < parts:
        whole = whole + lax.ppermute(whole, "inp", [(j, (j + step) % parts) for j in range(parts)])
        step *= 2
    return whole


def in_vmem(x, owners=2):
    return x if owners > 2 else pltpu.with_memory_space_constraint(x, pltpu.VMEM)


def body(volt, mask, table):
    owners = lax.axis_size("chan")
    slots = table.shape[0] // owners
    full_mask = gather_mask(mask)
    turned = lax.all_to_all(volt, "inp", split_axis=0, concat_axis=1, tiled=True)[0]
    turned, full_mask = lax.optimization_barrier((turned, full_mask))
    count, _, frames = turned.shape
    flat = in_vmem(turned.reshape(count, 2 * frames))
    me = lax.axis_index("chan").reshape(1)
    blocks = count // TB

    def shift(x, d):
        return lax.ppermute(x, "chan", [(j, (j + d) % owners) for j in range(owners)])

    sent = pl.pallas_call(
        functools.partial(sent_kernel, owners, slots),
        out_shape=[(pltpu.VMEM if owners == 2 else jax.ShapeDtypeStruct)((KPO, 2, TB, TB), jnp.float32)] * (owners - 1),
        in_specs=[SMEM, SMEM, VMEM],
        out_specs=[VMEM] * (owners - 1),
        name="sent",
    )(table, me, flat)
    arrived = [in_vmem(shift(sent[d - 1], d), owners) for d in range(1, owners)]

    gains, masked = pl.pallas_call(
        calibrate_kernel,
        out_shape=[
            jax.ShapeDtypeStruct((1, count), jnp.float32),
            pltpu.VMEM((blocks, TB), jnp.float32),
        ],
        in_specs=[VMEM] * 3,
        out_specs=[VMEM] * 2,
        name="calibrate",
    )(flat, full_mask, first_basis(count))
    other_gains = [in_vmem(shift(masked, d), owners) for d in range(1, owners)]

    vis_shape = jax.ShapeDtypeStruct((owners, KPO, 2, TB, TB), jnp.bfloat16)
    vis = pl.pallas_call(
        functools.partial(own_kernel, slots),
        out_shape=vis_shape,
        in_specs=[SMEM, SMEM, VMEM, VMEM],
        out_specs=ANY,
        scratch_shapes=[pltpu.VMEM((KPO, 2, TB, TB), jnp.bfloat16), pltpu.SemaphoreType.DMA],
        name="own",
    )(table, me, flat, masked)
    vis = pl.pallas_call(
        functools.partial(others_kernel, owners, slots),
        out_shape=vis_shape,
        in_specs=[SMEM, SMEM] + [VMEM] * (2 * owners - 2) + [ANY],
        out_specs=ANY,
        scratch_shapes=[
            pltpu.VMEM((owners - 1, KPO, 2, TB, TB), jnp.bfloat16),
            pltpu.SemaphoreType.DMA((owners - 1,)),
        ],
        input_output_aliases={2 * owners: 0},
        name="others",
    )(table, me, *arrived, *other_gains, vis)
    return (vis[None, :, None], gains.reshape(1, 1, count))


def solution(mesh):
    placed = (P("chan", "inp", None, None), P("inp"), P())
    return jax.shard_map(
        body,
        mesh=mesh,
        in_specs=placed,
        out_specs=(P("inp", None, "chan", None, None, None, None), P("chan", "inp", None)),
        check_vma=False,
    )
```

```python
import functools
import math

import jax
import jax.numpy as jnp
import numpy as np
from jax import lax
from jax.experimental import pallas as pl
from jax.experimental.pallas import tpu as pltpu
from jax.sharding import PartitionSpec as P

TB = 128
RANK = 4
ITERS = 8
KPO = 4
EPS = 1e-06
SPLITS = 2

VMEM = pl.BlockSpec(memory_space=pltpu.VMEM)
ANY = pl.BlockSpec(memory_space=pl.ANY)
SMEM = pl.BlockSpec(memory_space=pltpu.SMEM)


def first_basis(count):
    turns = np.outer(np.arange(RANK), np.arange(count)) % count
    angle = 2.0 * math.pi / count * turns
    both = np.concatenate([np.cos(angle), np.sin(angle)], axis=0)
    return (both / math.sqrt(count)).astype(np.float32)


def pieces(x):
    parts = []
    rest = x
    for k in range(SPLITS):
        part = rest.astype(jnp.bfloat16).astype(jnp.float32)
        parts.append(part)
        rest = rest - part
    return jnp.concatenate(parts, axis=0).astype(jnp.bfloat16)


def dot(x, y):
    split = lax.dot_general(x, y, (((1,), (0,)), ((), ())), preferred_element_type=jnp.float32)
    rows = split.shape[0] // SPLITS
    total = split[(SPLITS - 1) * rows :]
    for k in range(SPLITS - 2, -1, -1):
        total = total + split[k * rows : (k + 1) * rows]
    return total


def swap(x):
    return jnp.concatenate([x[RANK:], x[:RANK]], axis=0)


def inner(row_real, row_imag, z, turned):
    first = jnp.sum(z * row_real + turned * row_imag, axis=1, keepdims=True)
    second = jnp.sum(z * row_imag - turned * row_real, axis=1, keepdims=True)
    return first, second


def times(x, k, first, second):
    return x[k : k + 1] * first + x[RANK + k : RANK + k + 1] * second


def gram_schmidt(z, p, sign, order):
    turned = sign * swap(z)
    w = z
    scales = jnp.zeros((2 * RANK, 1), jnp.float32)
    for l in range(RANK):
        row_real = w[l : l + 1]
        row_imag = w[RANK + l : RANK + l + 1]
        norm = jnp.sum(row_real * row_real + row_imag * row_imag, axis=1, keepdims=True)
        scale = lax.rsqrt(norm + EPS)
        scales = jnp.where(order == l, scale, scales)
        if l < RANK - 1:
            first, second = inner(row_real, row_imag, z, turned)
            keep = jnp.where(order > l, scale * scale, 0.0)
            first, second = first * keep, second * keep
            w = w - times(w, l, first, second)
            p = p - times(p, l, first, second)
    return w * scales, p * scales


def calibrate_kernel(v_ref, mask_ref, basis_ref, gains_ref, masked_ref, vt_ref):
    _, count, frames = v_ref.shape
    mask = mask_ref[...].astype(jnp.float32)
    rows = lax.broadcasted_iota(jnp.int32, (2 * RANK, 1), 0)
    sign = jnp.where(rows < RANK, 1.0, -1.0)
    order = jnp.where(rows < RANK, rows, rows - RANK)
    for part in range(2):
        for k in range(0, count, 2 * TB):
            vt_ref[part, :, k : k + 2 * TB] = jnp.transpose(v_ref[part, k : k + 2 * TB, :])

    def project(q):
        x = pieces(q)
        return dot(x, v_ref[0]) + sign * swap(dot(x, v_ref[1]))

    def expand(y):
        z = dot(pieces(y), vt_ref[0]) - dot(pieces(sign * swap(y)), vt_ref[1])
        return z * (mask * (1.0 / frames))

    def step(_, z):
        return expand(gram_schmidt(z, project(z), sign, order)[1])

    z = lax.fori_loop(0, ITERS - 1, step, expand(project(basis_ref[...] * mask)))
    q, y = gram_schmidt(z, project(z), sign, order)
    turned = sign * swap(y)
    u = jnp.zeros_like(q)
    for k in range(RANK):
        u = u + times(q, k, *inner(y[k : k + 1], y[RANK + k : RANK + k + 1], y, turned))
    d = jnp.sum(u * q, axis=0, keepdims=True) * (1.0 / frames)
    floor = 0.1 * (jnp.sum(d, axis=1, keepdims=True) / count) + EPS
    gains = lax.rsqrt(jnp.maximum(d, floor))
    gains_ref[...] = gains
    masked = gains * mask
    for k in range(count // TB):
        masked_ref[k : k + 1, :] = masked[:, k * TB : (k + 1) * TB]


def product(v_ref, tile):
    _, count, frames = v_ref.shape
    blocks = count // TB
    row = pl.ds(pl.multiple_of((tile // blocks) * TB, TB), TB)
    col = pl.ds(pl.multiple_of(lax.rem(tile, blocks) * TB, TB), TB)
    real, imag = v_ref[0, row, :], v_ref[1, row, :]
    dims = (((1,), (1,)), ((), ()))
    both = lax.dot_general(
        jnp.concatenate([real, imag], axis=0), v_ref[0, col, :], dims, preferred_element_type=jnp.float32
    )
    both = both + lax.dot_general(
        jnp.concatenate([imag, -real], axis=0), v_ref[1, col, :], dims, preferred_element_type=jnp.float32
    )
    return both * (1.0 / frames)


def outer(gains_ref, tile):
    blocks = gains_ref.shape[0]
    row = gains_ref[pl.ds(tile // blocks, 1), :]
    col = gains_ref[pl.ds(lax.rem(tile, blocks), 1), :]
    return jnp.transpose(jnp.broadcast_to(row, (TB, TB))) * col


def sent_kernel(owners, slots, table_ref, me_ref, v_ref, *out_refs):
    for d in range(1, owners):
        owner = lax.rem(me_ref[0] + d, owners)
        for s in range(KPO):
            both = product(v_ref, table_ref[owner * slots + s])
            out_refs[d - 1][s, 0] = both[:TB]
            out_refs[d - 1][s, 1] = both[TB:]


def own_kernel(slots, table_ref, me_ref, v_ref, gains_ref, vis_ref, held, sem):
    me = me_ref[0]
    for s in range(KPO):
        tile = table_ref[me * slots + s]
        both = product(v_ref, tile)
        scale = outer(gains_ref, tile)
        held[s, 0] = (scale * both[:TB]).astype(jnp.bfloat16)
        held[s, 1] = (scale * both[TB:]).astype(jnp.bfloat16)
    copy = pltpu.make_async_copy(held, vis_ref.at[me], sem)
    copy.start()
    copy.wait()


def others_kernel(owners, slots, table_ref, me_ref, *refs):
    tile_refs, gain_refs = refs[: owners - 1], refs[owners - 1 : 2 * owners - 2]
    vis_ref, held, sem = refs[-3:]
    me = me_ref[0]
    copies = []
    for d in range(1, owners):
        for s in range(KPO):
            scale = outer(gain_refs[d - 1], table_ref[me * slots + s])
            for part in range(2):
                held[d - 1, s, part] = (scale * tile_refs[d - 1][s, part]).astype(jnp.bfloat16)
        source = lax.rem(me + owners - d, owners)
        copies.append(pltpu.make_async_copy(held.at[d - 1], vis_ref.at[source], sem.at[d - 1]))
        copies[-1].start()
    for copy in copies:
        copy.wait()


def digits(parts):
    stride = parts
    while stride > 1:
        radix = next(r for r in (4, 3, 2, stride) if stride % r == 0)
        stride //= radix
        yield stride, radix


def sum_digit(x, stride, radix):
    parts = lax.axis_size("inp")
    span = stride * radix
    moved = []
    for d in range(1, radix):
        pairs = [(j, j // span * span + (j + d * stride) % span) for j in range(parts)]
        moved.append(lax.ppermute(x, "inp", pairs))
    return sum(moved, x)


def in_vmem(x, owners=2):
    return x if owners > 2 else pltpu.with_memory_space_constraint(x, pltpu.VMEM)


def body(volt, mask, table):
    owners = lax.axis_size("chan")
    slots = table.shape[0] // owners
    parts, size = lax.axis_size("inp"), mask.shape[0]
    first, *later = digits(parts)
    full_mask = jnp.zeros((1, parts * size), mask.dtype)
    full_mask = lax.dynamic_update_slice(full_mask, mask.reshape(1, size), (0, lax.axis_index("inp") * size))
    full_mask = sum_digit(full_mask, *first)
    turned = lax.all_to_all(volt, "inp", split_axis=0, concat_axis=1, tiled=True)[0]
    turned, full_mask = lax.optimization_barrier((turned, full_mask))
    for digit in later:
        full_mask = sum_digit(full_mask, *digit)
    count, _, frames = turned.shape
    flat = in_vmem(jnp.transpose(turned, (1, 0, 2)))
    me = lax.axis_index("chan").reshape(1)
    blocks = count // TB

    def shift(x, d):
        return lax.ppermute(x, "chan", [(j, (j + d) % owners) for j in range(owners)])

    sent = pl.pallas_call(
        functools.partial(sent_kernel, owners, slots),
        out_shape=[(pltpu.VMEM if owners == 2 else jax.ShapeDtypeStruct)((KPO, 2, TB, TB), jnp.float32)] * (owners - 1),
        in_specs=[SMEM, SMEM, VMEM],
        out_specs=[VMEM] * (owners - 1),
        name="sent",
    )(table, me, flat)
    arrived = [in_vmem(shift(sent[d - 1], d), owners) for d in range(1, owners)]

    gains, masked = pl.pallas_call(
        calibrate_kernel,
        out_shape=[
            jax.ShapeDtypeStruct((1, count), jnp.float32),
            pltpu.VMEM((blocks, TB), jnp.float32),
        ],
        in_specs=[VMEM] * 3,
        out_specs=[VMEM] * 2,
        scratch_shapes=[pltpu.VMEM((2, frames, count), jnp.bfloat16)],
        name="calibrate",
    )(flat, in_vmem(full_mask), first_basis(count))
    other_gains = [in_vmem(shift(masked, d), owners) for d in range(1, owners)]

    vis_shape = jax.ShapeDtypeStruct((owners, KPO, 2, TB, TB), jnp.bfloat16)
    vis = pl.pallas_call(
        functools.partial(own_kernel, slots),
        out_shape=vis_shape,
        in_specs=[SMEM, SMEM, VMEM, VMEM],
        out_specs=ANY,
        scratch_shapes=[pltpu.VMEM((KPO, 2, TB, TB), jnp.bfloat16), pltpu.SemaphoreType.DMA],
        name="own",
    )(table, me, flat, masked)
    vis = pl.pallas_call(
        functools.partial(others_kernel, owners, slots),
        out_shape=vis_shape,
        in_specs=[SMEM, SMEM] + [VMEM] * (2 * owners - 2) + [ANY],
        out_specs=ANY,
        scratch_shapes=[
            pltpu.VMEM((owners - 1, KPO, 2, TB, TB), jnp.bfloat16),
            pltpu.SemaphoreType.DMA((owners - 1,)),
        ],
        input_output_aliases={2 * owners: 0},
        name="others",
    )(table, me, *arrived, *other_gains, vis)
    return (vis[None, :, None], gains.reshape(1, 1, count))


def solution(mesh):
    placed = (P("chan", "inp", None, None), P("inp"), P())
    return jax.shard_map(
        body,
        mesh=mesh,
        in_specs=placed,
        out_specs=(P("inp", None, "chan", None, None, None, None), P("chan", "inp", None)),
        check_vma=False,
    )
```

```python
import functools
import math

import jax
import jax.numpy as jnp
import numpy as np
from jax import lax
from jax.experimental import pallas as pl
from jax.experimental.pallas import tpu as pltpu
from jax.sharding import PartitionSpec as P

TB = 128
RANK = 4
ITERS = 8
KPO = 4
EPS = 1e-06
SPLITS = 2

VMEM = pl.BlockSpec(memory_space=pltpu.VMEM)
ANY = pl.BlockSpec(memory_space=pl.ANY)
SMEM = pl.BlockSpec(memory_space=pltpu.SMEM)


def first_basis(count):
    turns = np.outer(np.arange(RANK), np.arange(count)) % count
    angle = 2.0 * math.pi / count * turns
    both = np.concatenate([np.cos(angle), np.sin(angle)], axis=0)
    return (both / math.sqrt(count)).astype(np.float32)


def pieces(x):
    parts = []
    rest = x
    for k in range(SPLITS):
        part = rest.astype(jnp.bfloat16).astype(jnp.float32)
        parts.append(part)
        rest = rest - part
    return jnp.concatenate(parts, axis=0).astype(jnp.bfloat16)


def dot(x, y):
    split = lax.dot_general(x, y, (((1,), (0,)), ((), ())), preferred_element_type=jnp.float32)
    rows = split.shape[0] // SPLITS
    total = split[(SPLITS - 1) * rows :]
    for k in range(SPLITS - 2, -1, -1):
        total = total + split[k * rows : (k + 1) * rows]
    return total


def swap(x):
    return jnp.concatenate([x[RANK:], x[:RANK]], axis=0)


def inner(row_real, row_imag, z, turned):
    first = jnp.sum(z * row_real + turned * row_imag, axis=1, keepdims=True)
    second = jnp.sum(z * row_imag - turned * row_real, axis=1, keepdims=True)
    return first, second


def times(x, k, first, second):
    return x[k : k + 1] * first + x[RANK + k : RANK + k + 1] * second


def gram_schmidt(z, p, sign, order):
    turned = sign * swap(z)
    w = z
    scales = jnp.zeros((2 * RANK, 1), jnp.float32)
    for l in range(RANK):
        row_real = w[l : l + 1]
        row_imag = w[RANK + l : RANK + l + 1]
        norm = jnp.sum(row_real * row_real + row_imag * row_imag, axis=1, keepdims=True)
        scale = lax.rsqrt(norm + EPS)
        scales = jnp.where(order == l, scale, scales)
        if l < RANK - 1:
            first, second = inner(row_real, row_imag, z, turned)
            keep = jnp.where(order > l, scale * scale, 0.0)
            first, second = first * keep, second * keep
            w = w - times(w, l, first, second)
            p = p - times(p, l, first, second)
    return w * scales, p * scales


def calibrate_kernel(v_ref, basis_ref, gains_ref, blocks_ref, vt_ref):
    parts, _, size, frames = v_ref.shape
    count = parts * size
    rows = lax.broadcasted_iota(jnp.int32, (2 * RANK, 1), 0)
    sign = jnp.where(rows < RANK, 1.0, -1.0)
    order = jnp.where(rows < RANK, rows, rows - RANK)
    group = 2 * TB // size
    for part in range(2):
        for k in range(0, parts, group):
            rows_k = v_ref[k : k + group, part].reshape(group * size, frames)
            vt_ref[part, :, k * size : (k + group) * size] = jnp.transpose(rows_k)

    def project(q):
        x = pieces(q)
        real, imag = (v_ref[:, part].reshape(count, frames) for part in range(2))
        return dot(x, real) + sign * swap(dot(x, imag))

    def expand(y):
        z = dot(pieces(y), vt_ref[0]) - dot(pieces(sign * swap(y)), vt_ref[1])
        return z * (1.0 / frames)

    def step(_, z):
        return expand(gram_schmidt(z, project(z), sign, order)[1])

    z = lax.fori_loop(0, ITERS - 1, step, expand(project(basis_ref[...])))
    q, y = gram_schmidt(z, project(z), sign, order)
    turned = sign * swap(y)
    u = jnp.zeros_like(q)
    for k in range(RANK):
        u = u + times(q, k, *inner(y[k : k + 1], y[RANK + k : RANK + k + 1], y, turned))
    d = jnp.sum(u * q, axis=0, keepdims=True) * (1.0 / frames)
    floor = 0.1 * (jnp.sum(d, axis=1, keepdims=True) / count) + EPS
    gains = lax.rsqrt(jnp.maximum(d, floor))
    gains_ref[...] = gains
    for k in range(count // TB):
        blocks_ref[k : k + 1, :] = gains[:, k * TB : (k + 1) * TB]


def product(v_ref, tile):
    parts, _, size, frames = v_ref.shape
    blocks = parts * size // TB
    group = TB // size
    row = pl.ds((tile // blocks) * group, group)
    col = pl.ds(lax.rem(tile, blocks) * group, group)
    real, imag, col_real, col_imag = (v_ref[k, part].reshape(TB, frames) for k in (row, col) for part in range(2))
    dims = (((1,), (1,)), ((), ()))
    both = lax.dot_general(
        jnp.concatenate([real, imag], axis=0), col_real, dims, preferred_element_type=jnp.float32
    )
    both = both + lax.dot_general(
        jnp.concatenate([imag, -real], axis=0), col_imag, dims, preferred_element_type=jnp.float32
    )
    return both * (1.0 / frames)


def outer(gains_ref, tile):
    blocks = gains_ref.shape[0]
    row = gains_ref[pl.ds(tile // blocks, 1), :]
    col = gains_ref[pl.ds(lax.rem(tile, blocks), 1), :]
    return jnp.transpose(jnp.broadcast_to(row, (TB, TB))) * col


def sent_kernel(owners, slots, table_ref, me_ref, v_ref, *out_refs):
    for d in range(1, owners):
        owner = lax.rem(me_ref[0] + d, owners)
        for s in range(KPO):
            both = product(v_ref, table_ref[owner * slots + s])
            out_refs[d - 1][s, 0] = both[:TB]
            out_refs[d - 1][s, 1] = both[TB:]


def own_kernel(slots, table_ref, me_ref, v_ref, gains_ref, vis_ref, held, sem):
    me = me_ref[0]
    for s in range(KPO):
        tile = table_ref[me * slots + s]
        both = product(v_ref, tile)
        scale = outer(gains_ref, tile)
        held[s, 0] = (scale * both[:TB]).astype(jnp.bfloat16)
        held[s, 1] = (scale * both[TB:]).astype(jnp.bfloat16)
    copy = pltpu.make_async_copy(held, vis_ref.at[me], sem)
    copy.start()
    copy.wait()


def others_kernel(owners, slots, table_ref, me_ref, *refs):
    tile_refs, gain_refs = refs[: owners - 1], refs[owners - 1 : 2 * owners - 2]
    vis_ref, held, sem = refs[-3:]
    me = me_ref[0]
    copies = []
    for d in range(1, owners):
        for s in range(KPO):
            scale = outer(gain_refs[d - 1], table_ref[me * slots + s])
            for part in range(2):
                held[d - 1, s, part] = (scale * tile_refs[d - 1][s, part]).astype(jnp.bfloat16)
        source = lax.rem(me + owners - d, owners)
        copies.append(pltpu.make_async_copy(held.at[d - 1], vis_ref.at[source], sem.at[d - 1]))
        copies[-1].start()
    for copy in copies:
        copy.wait()


def in_vmem(x, owners=2):
    return x if owners > 2 else pltpu.with_memory_space_constraint(x, pltpu.VMEM)


def body(volt, mask, table):
    owners = lax.axis_size("chan")
    slots = table.shape[0] // owners
    masked = jnp.transpose(volt, (0, 2, 1, 3)) * mask.astype(jnp.bfloat16)[None, None, :, None]
    turned = lax.all_to_all(masked, "inp", split_axis=0, concat_axis=0, tiled=True)
    parts, _, size, frames = turned.shape
    count = parts * size
    flat = in_vmem(turned)
    me = lax.axis_index("chan").reshape(1)
    blocks = count // TB

    def shift(x, d):
        return lax.ppermute(x, "chan", [(j, (j + d) % owners) for j in range(owners)])

    sent = pl.pallas_call(
        functools.partial(sent_kernel, owners, slots),
        out_shape=[(pltpu.VMEM if owners == 2 else jax.ShapeDtypeStruct)((KPO, 2, TB, TB), jnp.float32)] * (owners - 1),
        in_specs=[SMEM, SMEM, VMEM],
        out_specs=[VMEM] * (owners - 1),
        name="sent",
    )(table, me, flat)
    arrived = [in_vmem(shift(sent[d - 1], d), owners) for d in range(1, owners)]

    gains, by_block = pl.pallas_call(
        calibrate_kernel,
        out_shape=[
            jax.ShapeDtypeStruct((1, count), jnp.float32),
            pltpu.VMEM((blocks, TB), jnp.float32),
        ],
        in_specs=[VMEM] * 2,
        out_specs=[VMEM] * 2,
        scratch_shapes=[pltpu.VMEM((2, frames, count), jnp.bfloat16)],
        name="calibrate",
    )(flat, first_basis(count))
    other_gains = [in_vmem(shift(by_block, d), owners) for d in range(1, owners)]

    vis_shape = jax.ShapeDtypeStruct((owners, KPO, 2, TB, TB), jnp.bfloat16)
    vis = pl.pallas_call(
        functools.partial(own_kernel, slots),
        out_shape=vis_shape,
        in_specs=[SMEM, SMEM, VMEM, VMEM],
        out_specs=ANY,
        scratch_shapes=[pltpu.VMEM((KPO, 2, TB, TB), jnp.bfloat16), pltpu.SemaphoreType.DMA],
        name="own",
    )(table, me, flat, by_block)
    vis = pl.pallas_call(
        functools.partial(others_kernel, owners, slots),
        out_shape=vis_shape,
        in_specs=[SMEM, SMEM] + [VMEM] * (2 * owners - 2) + [ANY],
        out_specs=ANY,
        scratch_shapes=[
            pltpu.VMEM((owners - 1, KPO, 2, TB, TB), jnp.bfloat16),
            pltpu.SemaphoreType.DMA((owners - 1,)),
        ],
        input_output_aliases={2 * owners: 0},
        name="others",
    )(table, me, *arrived, *other_gains, vis)
    return (vis[None, :, None], gains.reshape(1, 1, count))


def solution(mesh):
    placed = (P("chan", "inp", None, None), P("inp"), P())
    return jax.shard_map(
        body,
        mesh=mesh,
        in_specs=placed,
        out_specs=(P("inp", None, "chan", None, None, None, None), P("chan", "inp", None)),
        check_vma=False,
    )
```

```python
import functools
import math

import jax
import jax.numpy as jnp
import numpy as np
from jax import lax
from jax.experimental import pallas as pl
from jax.experimental.pallas import tpu as pltpu
from jax.sharding import PartitionSpec as P

TB = 128
RANK = 4
ITERS = 8
KPO = 4
EPS = 1e-06
LANES = 128
GROUP = 4
SPLITS = 2

VMEM = pl.BlockSpec(memory_space=pltpu.VMEM)
ANY = pl.BlockSpec(memory_space=pl.ANY)
HBM = pl.BlockSpec(memory_space=pltpu.HBM)
SMEM = pl.BlockSpec(memory_space=pltpu.SMEM)


def first_basis(count):
    turns = np.outer(np.arange(RANK), np.arange(count)) % count
    angle = 2.0 * math.pi / count * turns
    both = np.concatenate([np.cos(angle), np.sin(angle)], axis=0)
    return (both / math.sqrt(count)).astype(np.float32)


def pieces(x):
    parts = []
    rest = x
    for k in range(SPLITS):
        part = rest.astype(jnp.bfloat16).astype(jnp.float32)
        parts.append(part)
        rest = rest - part
    return jnp.concatenate(parts, axis=0).astype(jnp.bfloat16)


def dot(x, y):
    split = lax.dot_general(x, y, (((1,), (0,)), ((), ())), preferred_element_type=jnp.float32)
    rows = split.shape[0] // SPLITS
    total = split[(SPLITS - 1) * rows :]
    for k in range(SPLITS - 2, -1, -1):
        total = total + split[k * rows : (k + 1) * rows]
    return total


def swap(x):
    return jnp.concatenate([x[RANK:], x[:RANK]], axis=0)


def inner(row_real, row_imag, z, turned):
    first = jnp.sum(z * row_real + turned * row_imag, axis=1, keepdims=True)
    second = jnp.sum(z * row_imag - turned * row_real, axis=1, keepdims=True)
    return first, second


def times(x, k, first, second):
    return x[k : k + 1] * first + x[RANK + k : RANK + k + 1] * second


def gram_schmidt(z, p, sign, order):
    turned = sign * swap(z)
    w = z
    scales = jnp.zeros((2 * RANK, 1), jnp.float32)
    for l in range(RANK):
        row_real = w[l : l + 1]
        row_imag = w[RANK + l : RANK + l + 1]
        norm = jnp.sum(row_real * row_real + row_imag * row_imag, axis=1, keepdims=True)
        scale = lax.rsqrt(norm + EPS)
        scales = jnp.where(order == l, scale, scales)
        if l < RANK - 1:
            first, second = inner(row_real, row_imag, z, turned)
            keep = jnp.where(order > l, scale * scale, 0.0)
            first, second = first * keep, second * keep
            w = w - times(w, l, first, second)
            p = p - times(p, l, first, second)
    return w * scales, p * scales


def calibrate_kernel(v_ref, basis_ref, gains_ref, blocks_ref, vt_ref, first, sem):
    _, count, frames = v_ref.shape
    copy = pltpu.make_async_copy(basis_ref, first, sem)
    copy.start()
    rows = lax.broadcasted_iota(jnp.int32, (2 * RANK, 1), 0)
    sign = jnp.where(rows < RANK, 1.0, -1.0)
    order = jnp.where(rows < RANK, rows, rows - RANK)
    for part in range(2):
        for k in range(0, count, 2 * TB):
            vt_ref[part, :, k : k + 2 * TB] = jnp.transpose(v_ref[part, k : k + 2 * TB, :])

    def project(q):
        x = pieces(q)
        return dot(x, v_ref[0]) + sign * swap(dot(x, v_ref[1]))

    def expand(y):
        z = dot(pieces(y), vt_ref[0]) - dot(pieces(sign * swap(y)), vt_ref[1])
        return z * (1.0 / frames)

    def step(_, z):
        return expand(gram_schmidt(z, project(z), sign, order)[1])

    copy.wait()
    z = lax.fori_loop(0, ITERS - 1, step, expand(project(first[...])))
    q, y = gram_schmidt(z, project(z), sign, order)
    turned = sign * swap(y)
    u = jnp.zeros_like(q)
    for k in range(RANK):
        u = u + times(q, k, *inner(y[k : k + 1], y[RANK + k : RANK + k + 1], y, turned))
    d = jnp.sum(u * q, axis=0, keepdims=True) * (1.0 / frames)
    floor = 0.1 * (jnp.sum(d, axis=1, keepdims=True) / count) + EPS
    gains = lax.rsqrt(jnp.maximum(d, floor))
    gains_ref[...] = gains
    for k in range(count // TB):
        blocks_ref[k : k + 1, :] = gains[:, k * TB : (k + 1) * TB]


def product(v_ref, tile):
    _, count, frames = v_ref.shape
    blocks = count // TB
    row = pl.ds(pl.multiple_of((tile // blocks) * TB, TB), TB)
    col = pl.ds(pl.multiple_of(lax.rem(tile, blocks) * TB, TB), TB)
    real, imag, col_real, col_imag = (v_ref[part, k, :] for k in (row, col) for part in range(2))
    dims = (((1,), (1,)), ((), ()))
    both = lax.dot_general(
        jnp.concatenate([real, imag], axis=0), col_real, dims, preferred_element_type=jnp.float32
    )
    both = both + lax.dot_general(
        jnp.concatenate([imag, -real], axis=0), col_imag, dims, preferred_element_type=jnp.float32
    )
    return both * (1.0 / frames)


def outer(gains_ref, tile):
    blocks = gains_ref.shape[0]
    row = gains_ref[pl.ds(tile // blocks, 1), :]
    col = gains_ref[pl.ds(lax.rem(tile, blocks), 1), :]
    return jnp.transpose(jnp.broadcast_to(row, (TB, TB))) * col


def front_kernel(targets, per, me_ref, mask_ref, volt_ref, *refs):
    out_refs, (taken, flags, sem) = refs[: len(targets)], refs[len(targets) :]
    parts, size, frames = out_refs[0].shape
    cols = frames // LANES
    rows = per * cols * parts
    chunk = taken.shape[1]
    copies = []
    for k, d in enumerate(targets):
        start = pl.multiple_of(lax.bitwise_xor(me_ref[0], d) * chunk, chunk)
        copies.append(pltpu.make_async_copy(volt_ref.at[pl.ds(start, chunk)], taken.at[k], sem.at[k]))
        copies[-1].start()
    flag_copy = pltpu.make_async_copy(mask_ref, flags, sem.at[len(targets)])
    flag_copy.start()
    row = lax.broadcasted_iota(jnp.int32, (rows, rows), 0)
    col = lax.broadcasted_iota(jnp.int32, (rows, rows), 1)
    block = lax.div(row, per)
    source = (lax.rem(row, per) * cols + lax.rem(block, cols)) * parts + lax.div(block, cols)
    lane = lax.broadcasted_iota(jnp.int32, (size, rows), 1)
    place = lax.broadcasted_iota(jnp.int32, (size, rows), 0)
    flag_copy.wait()
    mask = flags[...].astype(jnp.bfloat16)
    selects = []
    for g in range(0, size, per):
        spread = (lax.div(lane, cols * parts) + g == place).astype(jnp.bfloat16)
        kept = jnp.dot(mask, spread, preferred_element_type=jnp.float32)
        selects.append(jnp.where(col == source, kept, 0.0).astype(jnp.bfloat16))
    for copy in copies:
        copy.wait()
    for k in range(len(targets)):
        for g, select in enumerate(selects):
            x = taken[k, g * rows : (g + 1) * rows, :]
            y = jnp.dot(select, x, preferred_element_type=jnp.float32).astype(jnp.bfloat16)
            for p in range(parts):
                for c in range(cols):
                    at = (p * cols + c) * per
                    out_refs[k][p, g * per : (g + 1) * per, c * LANES : (c + 1) * LANES] = y[at : at + per]


def join_kernel(order, me_ref, *refs):
    v_ref = refs[-1]
    size = refs[0].shape[1]
    for d, block_ref in zip(order, refs[:-1]):
        start = pl.multiple_of(lax.bitwise_xor(me_ref[0], d) * size, size)
        v_ref[:, pl.ds(start, size), :] = block_ref[...]


def corner_turn(volt, mask):
    parts = lax.axis_size("inp")
    _, size, both, frames = volt.shape
    me = lax.axis_index("inp").reshape(1)
    cols = frames // LANES
    chunk = size * cols * both
    rows = volt.reshape(parts, size, both, cols, LANES).transpose(0, 1, 3, 2, 4).reshape(parts * chunk, LANES)
    near = list(range(1, parts // 2))
    far = list(range(parts // 2, parts))
    order = [far[0]]
    for k in range(len(near)):
        order += [far[k + 1], near[k]]
    order.append(0)
    shape = (both, size, frames)
    blocks = []
    groups = [order[at : at + GROUP] for at in range(0, parts, GROUP)]
    order = sum(reversed(groups), [])
    for at in range(0, parts, GROUP):
        targets = order[at : at + GROUP]
        fronts = pl.pallas_call(
            functools.partial(front_kernel, targets, min(size, 16)),
            out_shape=[small(parts)(shape, volt.dtype)] * len(targets),
            in_specs=[SMEM, HBM, HBM],
            out_specs=[VMEM] * len(targets),
            scratch_shapes=[
                pltpu.VMEM((len(targets), chunk, LANES), volt.dtype),
                pltpu.VMEM((1, size), mask.dtype),
                pltpu.SemaphoreType.DMA((len(targets) + 1,)),
            ],
            compiler_params=pltpu.CompilerParams(vmem_limit_bytes=8 << 20),
            name="front",
        )(me, in_hbm(mask.reshape(1, size)), in_hbm(rows))
        for d, block in zip(targets, fronts):
            pairs = [(j, j ^ d) for j in range(parts)]
            blocks.append(lax.ppermute(block, "inp", pairs) if d else block)
    return pl.pallas_call(
        functools.partial(join_kernel, order),
        out_shape=pltpu.VMEM((both, parts * size, frames), volt.dtype),
        in_specs=[SMEM] + [VMEM] * parts,
        out_specs=VMEM,
        compiler_params=pltpu.CompilerParams(vmem_limit_bytes=4 << 20),
        name="join",
    )(me, *[in_vmem(block, parts // 8) for block in blocks])


def in_hbm(x):
    return pltpu.with_memory_space_constraint(x, pltpu.HBM)


def small(parts):
    return pltpu.VMEM if parts <= 16 else jax.ShapeDtypeStruct


def sent_kernel(owners, slots, table_ref, me_ref, v_ref, *out_refs):
    for d in range(1, owners):
        owner = lax.rem(me_ref[0] + d, owners)
        for s in range(KPO):
            both = product(v_ref, table_ref[owner * slots + s])
            out_refs[d - 1][s, 0] = both[:TB]
            out_refs[d - 1][s, 1] = both[TB:]


def own_kernel(slots, table_ref, me_ref, v_ref, gains_ref, vis_ref, held, sem):
    me = me_ref[0]
    for s in range(KPO):
        tile = table_ref[me * slots + s]
        both = product(v_ref, tile)
        scale = outer(gains_ref, tile)
        held[s, 0] = (scale * both[:TB]).astype(jnp.bfloat16)
        held[s, 1] = (scale * both[TB:]).astype(jnp.bfloat16)
    copy = pltpu.make_async_copy(held, vis_ref.at[me], sem)
    copy.start()
    copy.wait()


def others_kernel(owners, slots, table_ref, me_ref, *refs):
    tile_refs, gain_refs = refs[: owners - 1], refs[owners - 1 : 2 * owners - 2]
    vis_ref, held, sem = refs[-3:]
    me = me_ref[0]
    copies = []
    for d in range(1, owners):
        for s in range(KPO):
            scale = outer(gain_refs[d - 1], table_ref[me * slots + s])
            for part in range(2):
                held[d - 1, s, part] = (scale * tile_refs[d - 1][s, part]).astype(jnp.bfloat16)
        source = lax.rem(me + owners - d, owners)
        copies.append(pltpu.make_async_copy(held.at[d - 1], vis_ref.at[source], sem.at[d - 1]))
        copies[-1].start()
    for copy in copies:
        copy.wait()


def in_vmem(x, owners=2):
    return x if owners > 2 else pltpu.with_memory_space_constraint(x, pltpu.VMEM)


def body(volt, mask, table):
    owners = lax.axis_size("chan")
    slots = table.shape[0] // owners
    flat = in_vmem(corner_turn(volt, mask))
    _, count, frames = flat.shape
    me = lax.axis_index("chan").reshape(1)
    blocks = count // TB

    def shift(x, d):
        return lax.ppermute(x, "chan", [(j, (j + d) % owners) for j in range(owners)])

    sent = pl.pallas_call(
        functools.partial(sent_kernel, owners, slots),
        out_shape=[(pltpu.VMEM if owners == 2 else jax.ShapeDtypeStruct)((KPO, 2, TB, TB), jnp.float32)] * (owners - 1),
        in_specs=[SMEM, SMEM, VMEM],
        out_specs=[VMEM] * (owners - 1),
        compiler_params=pltpu.CompilerParams(vmem_limit_bytes=12 << 20),
        name="sent",
    )(table, me, flat)
    arrived = [in_vmem(shift(sent[d - 1], d), owners) for d in range(1, owners)]

    gains, by_block = pl.pallas_call(
        calibrate_kernel,
        out_shape=[
            jax.ShapeDtypeStruct((1, count), jnp.float32),
            pltpu.VMEM((blocks, TB), jnp.float32),
        ],
        in_specs=[VMEM, HBM],
        out_specs=[VMEM] * 2,
        scratch_shapes=[
            pltpu.VMEM((2, frames, count), jnp.bfloat16),
            pltpu.VMEM((2 * RANK, count), jnp.float32),
            pltpu.SemaphoreType.DMA,
        ],
        compiler_params=pltpu.CompilerParams(vmem_limit_bytes=12 << 20),
        name="calibrate",
    )(flat, in_hbm(jnp.asarray(first_basis(count))))
    other_gains = [in_vmem(shift(by_block, d), owners) for d in range(1, owners)]

    vis_shape = jax.ShapeDtypeStruct((owners, KPO, 2, TB, TB), jnp.bfloat16)
    vis = pl.pallas_call(
        functools.partial(own_kernel, slots),
        out_shape=vis_shape,
        in_specs=[SMEM, SMEM, VMEM, VMEM],
        out_specs=ANY,
        scratch_shapes=[pltpu.VMEM((KPO, 2, TB, TB), jnp.bfloat16), pltpu.SemaphoreType.DMA],
        compiler_params=pltpu.CompilerParams(vmem_limit_bytes=12 << 20),
        name="own",
    )(table, me, flat, by_block)
    vis = pl.pallas_call(
        functools.partial(others_kernel, owners, slots),
        out_shape=vis_shape,
        in_specs=[SMEM, SMEM] + [VMEM] * (2 * owners - 2) + [ANY],
        out_specs=ANY,
        scratch_shapes=[
            pltpu.VMEM((owners - 1, KPO, 2, TB, TB), jnp.bfloat16),
            pltpu.SemaphoreType.DMA((owners - 1,)),
        ],
        input_output_aliases={2 * owners: 0},
        compiler_params=pltpu.CompilerParams(vmem_limit_bytes=12 << 20),
        name="others",
    )(table, me, *arrived, *other_gains, vis)
    return (vis[None, :, None], gains.reshape(1, 1, count))


def solution(mesh):
    placed = (P("chan", "inp", None, None), P("inp"), P())
    return jax.shard_map(
        body,
        mesh=mesh,
        in_specs=placed,
        out_specs=(P("inp", None, "chan", None, None, None, None), P("chan", "inp", None)),
        check_vma=False,
    )
```

```python
import functools
import math

import jax
import jax.numpy as jnp
import numpy as np
from jax import lax
from jax.experimental import pallas as pl
from jax.experimental.pallas import tpu as pltpu
from jax.sharding import PartitionSpec as P

TB = 128
RANK = 4
ITERS = 8
KPO = 4
EPS = 1e-06
LANES = 128
GROUP = 4
FIRST = 2
SPLITS = 2

VMEM = pl.BlockSpec(memory_space=pltpu.VMEM)
ANY = pl.BlockSpec(memory_space=pl.ANY)
HBM = pl.BlockSpec(memory_space=pltpu.HBM)
SMEM = pl.BlockSpec(memory_space=pltpu.SMEM)


def first_basis(count):
    turns = np.outer(np.arange(RANK), np.arange(count)) % count
    angle = 2.0 * math.pi / count * turns
    both = np.concatenate([np.cos(angle), np.sin(angle)], axis=0)
    return (both / math.sqrt(count)).astype(np.float32)


def pieces(x):
    parts = []
    rest = x
    for k in range(SPLITS):
        part = rest.astype(jnp.bfloat16).astype(jnp.float32)
        parts.append(part)
        rest = rest - part
    return jnp.concatenate(parts, axis=0).astype(jnp.bfloat16)


def dot(x, y):
    split = lax.dot_general(x, y, (((1,), (0,)), ((), ())), preferred_element_type=jnp.float32)
    rows = split.shape[0] // SPLITS
    total = split[(SPLITS - 1) * rows :]
    for k in range(SPLITS - 2, -1, -1):
        total = total + split[k * rows : (k + 1) * rows]
    return total


def swap(x):
    return jnp.concatenate([x[RANK:], x[:RANK]], axis=0)


def inner(row_real, row_imag, z, turned):
    first = jnp.sum(z * row_real + turned * row_imag, axis=1, keepdims=True)
    second = jnp.sum(z * row_imag - turned * row_real, axis=1, keepdims=True)
    return first, second


def times(x, k, first, second):
    return x[k : k + 1] * first + x[RANK + k : RANK + k + 1] * second


def gram_schmidt(z, p, sign, order):
    turned = sign * swap(z)
    w = z
    scales = jnp.zeros((2 * RANK, 1), jnp.float32)
    for l in range(RANK):
        row_real = w[l : l + 1]
        row_imag = w[RANK + l : RANK + l + 1]
        norm = jnp.sum(row_real * row_real + row_imag * row_imag, axis=1, keepdims=True)
        scale = lax.rsqrt(norm + EPS)
        scales = jnp.where(order == l, scale, scales)
        if l < RANK - 1:
            first, second = inner(row_real, row_imag, z, turned)
            keep = jnp.where(order > l, scale * scale, 0.0)
            first, second = first * keep, second * keep
            w = w - times(w, l, first, second)
            p = p - times(p, l, first, second)
    return w * scales, p * scales


def calibrate_kernel(v_ref, first, gains_ref, blocks_ref, vt_ref):
    _, count, frames = v_ref.shape
    rows = lax.broadcasted_iota(jnp.int32, (2 * RANK, 1), 0)
    sign = jnp.where(rows < RANK, 1.0, -1.0)
    order = jnp.where(rows < RANK, rows, rows - RANK)
    for part in range(2):
        for k in range(0, count, 2 * TB):
            vt_ref[part, :, k : k + 2 * TB] = jnp.transpose(v_ref[part, k : k + 2 * TB, :])

    def project(q):
        x = pieces(q)
        return dot(x, v_ref[0]) + sign * swap(dot(x, v_ref[1]))

    def expand(y):
        z = dot(pieces(y), vt_ref[0]) - dot(pieces(sign * swap(y)), vt_ref[1])
        return z * (1.0 / frames)

    def step(_, z):
        return expand(gram_schmidt(z, project(z), sign, order)[1])

    z = lax.fori_loop(0, ITERS - 1, step, expand(project(first[...])))
    q, y = gram_schmidt(z, project(z), sign, order)
    turned = sign * swap(y)
    u = jnp.zeros_like(q)
    for k in range(RANK):
        u = u + times(q, k, *inner(y[k : k + 1], y[RANK + k : RANK + k + 1], y, turned))
    d = jnp.sum(u * q, axis=0, keepdims=True) * (1.0 / frames)
    floor = 0.1 * (jnp.sum(d, axis=1, keepdims=True) / count) + EPS
    gains = lax.rsqrt(jnp.maximum(d, floor))
    gains_ref[...] = gains
    for k in range(count // TB):
        blocks_ref[k : k + 1, :] = gains[:, k * TB : (k + 1) * TB]


def product(v_ref, tile):
    _, count, frames = v_ref.shape
    blocks = count // TB
    row = pl.ds(pl.multiple_of((tile // blocks) * TB, TB), TB)
    col = pl.ds(pl.multiple_of(lax.rem(tile, blocks) * TB, TB), TB)
    real, imag, col_real, col_imag = (v_ref[part, k, :] for k in (row, col) for part in range(2))
    dims = (((1,), (1,)), ((), ()))
    both = lax.dot_general(
        jnp.concatenate([real, imag], axis=0), col_real, dims, preferred_element_type=jnp.float32
    )
    both = both + lax.dot_general(
        jnp.concatenate([imag, -real], axis=0), col_imag, dims, preferred_element_type=jnp.float32
    )
    return both * (1.0 / frames)


def outer(gains_ref, tile):
    blocks = gains_ref.shape[0]
    row = gains_ref[pl.ds(tile // blocks, 1), :]
    col = gains_ref[pl.ds(lax.rem(tile, blocks), 1), :]
    return jnp.transpose(jnp.broadcast_to(row, (TB, TB))) * col


def front_kernel(targets, per, me_ref, mask_ref, volt_ref, *refs):
    out_refs, (taken, flags, sem) = refs[: len(targets)], refs[len(targets) :]
    parts, size, frames = out_refs[0].shape
    cols = frames // LANES
    rows = per * cols * parts
    chunk = taken.shape[1]
    copies = []
    for k, d in enumerate(targets):
        start = pl.multiple_of(lax.bitwise_xor(me_ref[0], d) * chunk, chunk)
        copies.append(pltpu.make_async_copy(volt_ref.at[pl.ds(start, chunk)], taken.at[k], sem.at[k]))
        copies[-1].start()
    flag_copy = pltpu.make_async_copy(mask_ref, flags, sem.at[len(targets)])
    flag_copy.start()
    row = lax.broadcasted_iota(jnp.int32, (rows, rows), 0)
    col = lax.broadcasted_iota(jnp.int32, (rows, rows), 1)
    block = lax.div(row, per)
    source = (lax.rem(row, per) * cols + lax.rem(block, cols)) * parts + lax.div(block, cols)
    lane = lax.broadcasted_iota(jnp.int32, (size, rows), 1)
    place = lax.broadcasted_iota(jnp.int32, (size, rows), 0)
    flag_copy.wait()
    mask = flags[...].astype(jnp.bfloat16)
    selects = []
    for g in range(0, size, per):
        spread = (lax.div(lane, cols * parts) + g == place).astype(jnp.bfloat16)
        kept = jnp.dot(mask, spread, preferred_element_type=jnp.float32)
        selects.append(jnp.where(col == source, kept, 0.0).astype(jnp.bfloat16))
    for copy in copies:
        copy.wait()
    for k in range(len(targets)):
        for g, select in enumerate(selects):
            x = taken[k, g * rows : (g + 1) * rows, :]
            y = jnp.dot(select, x, preferred_element_type=jnp.float32).astype(jnp.bfloat16)
            for p in range(parts):
                for c in range(cols):
                    at = (p * cols + c) * per
                    out_refs[k][p, g * per : (g + 1) * per, c * LANES : (c + 1) * LANES] = y[at : at + per]


def join_kernel(order, me_ref, *refs):
    v_ref = refs[-1]
    size = refs[0].shape[1]
    for d, block_ref in zip(order, refs[:-1]):
        start = pl.multiple_of(lax.bitwise_xor(me_ref[0], d) * size, size)
        v_ref[:, pl.ds(start, size), :] = block_ref[...]


def corner_turn(volt, mask):
    parts = lax.axis_size("inp")
    _, size, both, frames = volt.shape
    me = lax.axis_index("inp").reshape(1)
    cols = frames // LANES
    chunk = size * cols * both
    rows = volt.reshape(parts, size, both, cols, LANES).transpose(0, 1, 3, 2, 4).reshape(parts * chunk, LANES)
    far = list(range(parts // 2, parts))
    near = sorted(range(1, parts // 2), key=lambda d: (-d.bit_length(), d))
    order = far[:1]
    for d, other in zip(near, far[1:]):
        order += [other, d]
    order.append(0)
    shape = (both, size, frames)
    blocks = []
    cuts = [0, *range(FIRST, GROUP, FIRST), *range(GROUP, parts, GROUP), parts]
    groups = [order[start:stop] for start, stop in zip(cuts, cuts[1:])][::-1]
    for targets in groups:
        fronts = pl.pallas_call(
            functools.partial(front_kernel, targets, min(size, 16)),
            out_shape=[small(parts)(shape, volt.dtype)] * len(targets),
            in_specs=[SMEM, HBM, HBM],
            out_specs=[VMEM] * len(targets),
            scratch_shapes=[
                pltpu.VMEM((len(targets), chunk, LANES), volt.dtype),
                pltpu.VMEM((1, size), mask.dtype),
                pltpu.SemaphoreType.DMA((len(targets) + 1,)),
            ],
            compiler_params=pltpu.CompilerParams(vmem_limit_bytes=8 << 20),
            name="front",
        )(me, in_hbm(mask.reshape(1, size)), in_hbm(rows))
        for d, block in zip(targets, fronts):
            pairs = [(j, j ^ d) for j in range(parts)]
            blocks.append(lax.ppermute(block, "inp", pairs) if d else block)
    return pl.pallas_call(
        functools.partial(join_kernel, sum(groups, [])),
        out_shape=pltpu.VMEM((both, parts * size, frames), volt.dtype),
        in_specs=[SMEM] + [VMEM] * parts,
        out_specs=VMEM,
        compiler_params=pltpu.CompilerParams(vmem_limit_bytes=4 << 20),
        name="join",
    )(me, *[in_vmem(block, parts // 8) for block in blocks])


def in_hbm(x):
    return pltpu.with_memory_space_constraint(x, pltpu.HBM)


def small(parts):
    return pltpu.VMEM if parts <= 16 else jax.ShapeDtypeStruct


def sent_kernel(owners, slots, table_ref, me_ref, v_ref, *out_refs):
    for d in range(1, owners):
        owner = lax.rem(me_ref[0] + d, owners)
        for s in range(KPO):
            both = product(v_ref, table_ref[owner * slots + s])
            out_refs[d - 1][s, 0] = both[:TB]
            out_refs[d - 1][s, 1] = both[TB:]


def own_kernel(slots, table_ref, me_ref, v_ref, gains_ref, vis_ref, held, sem):
    me = me_ref[0]
    for s in range(KPO):
        tile = table_ref[me * slots + s]
        both = product(v_ref, tile)
        scale = outer(gains_ref, tile)
        held[s, 0] = (scale * both[:TB]).astype(jnp.bfloat16)
        held[s, 1] = (scale * both[TB:]).astype(jnp.bfloat16)
    copy = pltpu.make_async_copy(held, vis_ref.at[me], sem)
    copy.start()
    copy.wait()


def others_kernel(owners, slots, table_ref, me_ref, *refs):
    tile_refs, gain_refs = refs[: owners - 1], refs[owners - 1 : 2 * owners - 2]
    vis_ref, held, sem = refs[-3:]
    me = me_ref[0]
    copies = []
    for d in range(1, owners):
        source = lax.rem(me + owners - d, owners)
        for s in range(KPO):
            scale = outer(gain_refs[d - 1], table_ref[me * slots + s])
            for part in range(2):
                held[d - 1, s, part] = (scale * tile_refs[d - 1][s, part]).astype(jnp.bfloat16)
            copies.append(pltpu.make_async_copy(held.at[d - 1, s], vis_ref.at[source, s], sem.at[d - 1, s]))
            copies[-1].start()
    for copy in copies:
        copy.wait()


def in_vmem(x, owners=2):
    return x if owners > 2 else pltpu.with_memory_space_constraint(x, pltpu.VMEM)


def body(volt, mask, table):
    owners = lax.axis_size("chan")
    slots = table.shape[0] // owners
    flat = in_vmem(corner_turn(volt, mask))
    _, count, frames = flat.shape
    me = lax.axis_index("chan").reshape(1)
    table = in_hbm(table)
    blocks = count // TB

    def shift(x, d):
        return lax.ppermute(x, "chan", [(j, (j + d) % owners) for j in range(owners)])

    sent = pl.pallas_call(
        functools.partial(sent_kernel, owners, slots),
        out_shape=[(pltpu.VMEM if owners == 2 else jax.ShapeDtypeStruct)((KPO, 2, TB, TB), jnp.float32)] * (owners - 1),
        in_specs=[SMEM, SMEM, VMEM],
        out_specs=[VMEM] * (owners - 1),
        compiler_params=pltpu.CompilerParams(vmem_limit_bytes=12 << 20),
        name="sent",
    )(table, me, flat)
    arrived = [in_vmem(shift(sent[d - 1], d), owners) for d in range(1, owners)]

    gains, by_block = pl.pallas_call(
        calibrate_kernel,
        out_shape=[
            jax.ShapeDtypeStruct((1, count), jnp.float32),
            pltpu.VMEM((blocks, TB), jnp.float32),
        ],
        in_specs=[VMEM, VMEM],
        out_specs=[VMEM] * 2,
        scratch_shapes=[pltpu.VMEM((2, frames, count), jnp.bfloat16)],
        compiler_params=pltpu.CompilerParams(vmem_limit_bytes=12 << 20),
        name="calibrate",
    )(flat, in_vmem(jnp.asarray(first_basis(count))))
    other_gains = [in_vmem(shift(by_block, d), owners) for d in range(1, owners)]

    vis_shape = jax.ShapeDtypeStruct((owners, KPO, 2, TB, TB), jnp.bfloat16)
    vis = pl.pallas_call(
        functools.partial(own_kernel, slots),
        out_shape=vis_shape,
        in_specs=[SMEM, SMEM, VMEM, VMEM],
        out_specs=ANY,
        scratch_shapes=[pltpu.VMEM((KPO, 2, TB, TB), jnp.bfloat16), pltpu.SemaphoreType.DMA],
        compiler_params=pltpu.CompilerParams(vmem_limit_bytes=12 << 20),
        name="own",
    )(table, me, flat, by_block)
    vis = pl.pallas_call(
        functools.partial(others_kernel, owners, slots),
        out_shape=vis_shape,
        in_specs=[SMEM, SMEM] + [VMEM] * (2 * owners - 2) + [ANY],
        out_specs=ANY,
        scratch_shapes=[
            pltpu.VMEM((owners - 1, KPO, 2, TB, TB), jnp.bfloat16),
            pltpu.SemaphoreType.DMA((owners - 1, KPO)),
        ],
        input_output_aliases={2 * owners: 0},
        compiler_params=pltpu.CompilerParams(vmem_limit_bytes=12 << 20),
        name="others",
    )(table, me, *arrived, *other_gains, vis)
    return (vis[None, :, None], gains.reshape(1, 1, count))


def solution(mesh):
    placed = (P("chan", "inp", None, None), P("inp"), P())
    return jax.shard_map(
        body,
        mesh=mesh,
        in_specs=placed,
        out_specs=(P("inp", None, "chan", None, None, None, None), P("chan", "inp", None)),
        check_vma=False,
    )
```

```python
import functools
import math

import jax
import jax.numpy as jnp
import numpy as np
from jax import lax
from jax.experimental import pallas as pl
from jax.experimental.pallas import tpu as pltpu
from jax.sharding import PartitionSpec as P

TB = 128
RANK = 4
ITERS = 8
KPO = 4
EPS = 1e-06
LANES = 128
GROUP = 4
FIRST = 2
RAW = 3
SPLITS = 2

VMEM = pl.BlockSpec(memory_space=pltpu.VMEM)
ANY = pl.BlockSpec(memory_space=pl.ANY)
HBM = pl.BlockSpec(memory_space=pltpu.HBM)
SMEM = pl.BlockSpec(memory_space=pltpu.SMEM)


def first_basis(count):
    turns = np.outer(np.arange(RANK), np.arange(count)) % count
    angle = 2.0 * math.pi / count * turns
    both = np.concatenate([np.cos(angle), np.sin(angle)], axis=0)
    return (both / math.sqrt(count)).astype(np.float32)


def pieces(x):
    parts = []
    rest = x
    for k in range(SPLITS):
        part = rest.astype(jnp.bfloat16).astype(jnp.float32)
        parts.append(part)
        rest = rest - part
    return jnp.concatenate(parts, axis=0).astype(jnp.bfloat16)


def dot(x, y):
    split = lax.dot_general(x, y, (((1,), (0,)), ((), ())), preferred_element_type=jnp.float32)
    rows = split.shape[0] // SPLITS
    total = split[(SPLITS - 1) * rows :]
    for k in range(SPLITS - 2, -1, -1):
        total = total + split[k * rows : (k + 1) * rows]
    return total


def swap(x):
    return jnp.concatenate([x[RANK:], x[:RANK]], axis=0)


def inner(row_real, row_imag, z, turned):
    first = jnp.sum(z * row_real + turned * row_imag, axis=1, keepdims=True)
    second = jnp.sum(z * row_imag - turned * row_real, axis=1, keepdims=True)
    return first, second


def times(x, k, first, second):
    return x[k : k + 1] * first + x[RANK + k : RANK + k + 1] * second


def gram_schmidt(z, p, sign, order):
    turned = sign * swap(z)
    w = z
    scales = jnp.zeros((2 * RANK, 1), jnp.float32)
    for l in range(RANK):
        row_real = w[l : l + 1]
        row_imag = w[RANK + l : RANK + l + 1]
        norm = jnp.sum(row_real * row_real + row_imag * row_imag, axis=1, keepdims=True)
        scale = lax.rsqrt(norm + EPS)
        scales = jnp.where(order == l, scale, scales)
        if l < RANK - 1:
            first, second = inner(row_real, row_imag, z, turned)
            keep = jnp.where(order > l, scale * scale, 0.0)
            first, second = first * keep, second * keep
            w = w - times(w, l, first, second)
            p = p - times(p, l, first, second)
    return w * scales, p * scales


def calibrate_kernel(owners, slots, table_ref, me_ref, v_ref, first, gains_ref, blocks_ref, *refs):
    ready_refs, vt_ref = refs[:-1], refs[-1]
    _, count, frames = v_ref.shape
    rows = lax.broadcasted_iota(jnp.int32, (2 * RANK, 1), 0)
    sign = jnp.where(rows < RANK, 1.0, -1.0)
    order = jnp.where(rows < RANK, rows, rows - RANK)
    for part in range(2):
        for k in range(0, count, 2 * TB):
            vt_ref[part, :, k : k + 2 * TB] = jnp.transpose(v_ref[part, k : k + 2 * TB, :])

    def project(q):
        x = pieces(q)
        return dot(x, v_ref[0]) + sign * swap(dot(x, v_ref[1]))

    def expand(y):
        z = dot(pieces(y), vt_ref[0]) - dot(pieces(sign * swap(y)), vt_ref[1])
        return z * (1.0 / frames)

    def step(_, z):
        return expand(gram_schmidt(z, project(z), sign, order)[1])

    z = lax.fori_loop(0, ITERS - 1, step, expand(project(first[...])))
    q, y = gram_schmidt(z, project(z), sign, order)
    turned = sign * swap(y)
    u = jnp.zeros_like(q)
    for k in range(RANK):
        u = u + times(q, k, *inner(y[k : k + 1], y[RANK + k : RANK + k + 1], y, turned))
    d = jnp.sum(u * q, axis=0, keepdims=True) * (1.0 / frames)
    floor = 0.1 * (jnp.sum(d, axis=1, keepdims=True) / count) + EPS
    gains = lax.rsqrt(jnp.maximum(d, floor))
    gains_ref[...] = gains
    for k in range(count // TB):
        blocks_ref[k : k + 1, :] = gains[:, k * TB : (k + 1) * TB]
    for d in range(1, owners):
        owner = lax.rem(me_ref[0] + d, owners)
        for s in range(RAW, KPO):
            tile = table_ref[owner * slots + s]
            both = product(v_ref, tile)
            scale = outer(blocks_ref, tile)
            ready_refs[d - 1][s - RAW, 0] = (scale * both[:TB]).astype(jnp.bfloat16)
            ready_refs[d - 1][s - RAW, 1] = (scale * both[TB:]).astype(jnp.bfloat16)


def product(v_ref, tile):
    _, count, frames = v_ref.shape
    blocks = count // TB
    row = pl.ds(pl.multiple_of((tile // blocks) * TB, TB), TB)
    col = pl.ds(pl.multiple_of(lax.rem(tile, blocks) * TB, TB), TB)
    real, imag, col_real, col_imag = (v_ref[part, k, :] for k in (row, col) for part in range(2))
    dims = (((1,), (1,)), ((), ()))
    both = lax.dot_general(
        jnp.concatenate([real, imag], axis=0), col_real, dims, preferred_element_type=jnp.float32
    )
    both = both + lax.dot_general(
        jnp.concatenate([imag, -real], axis=0), col_imag, dims, preferred_element_type=jnp.float32
    )
    return both * (1.0 / frames)


def outer(gains_ref, tile):
    blocks = gains_ref.shape[0]
    row = gains_ref[pl.ds(tile // blocks, 1), :]
    col = gains_ref[pl.ds(lax.rem(tile, blocks), 1), :]
    return jnp.transpose(jnp.broadcast_to(row, (TB, TB))) * col


def front_kernel(targets, per, me_ref, mask_ref, volt_ref, *refs):
    if 0 in targets:
        table_ref, *refs = refs
        staged_ref = refs.pop(len(targets))
    out_refs, (taken, flags, sem) = refs[: len(targets)], refs[len(targets) :]
    parts, size, frames = out_refs[0].shape
    cols = frames // LANES
    rows = per * cols * parts
    chunk = taken.shape[1]
    copies = []
    for k, d in enumerate(targets):
        start = pl.multiple_of(lax.bitwise_xor(me_ref[0], d) * chunk, chunk)
        copies.append(pltpu.make_async_copy(volt_ref.at[pl.ds(start, chunk)], taken.at[k], sem.at[k]))
        copies[-1].start()
    flag_copy = pltpu.make_async_copy(mask_ref, flags, sem.at[len(targets)])
    flag_copy.start()
    if 0 in targets:
        copies.append(pltpu.make_async_copy(table_ref, staged_ref, sem.at[len(targets) + 1]))
        copies[-1].start()
    row = lax.broadcasted_iota(jnp.int32, (rows, rows), 0)
    col = lax.broadcasted_iota(jnp.int32, (rows, rows), 1)
    block = lax.div(row, per)
    source = (lax.rem(row, per) * cols + lax.rem(block, cols)) * parts + lax.div(block, cols)
    lane = lax.broadcasted_iota(jnp.int32, (size, rows), 1)
    place = lax.broadcasted_iota(jnp.int32, (size, rows), 0)
    flag_copy.wait()
    mask = flags[...].astype(jnp.bfloat16)
    selects = []
    for g in range(0, size, per):
        spread = (lax.div(lane, cols * parts) + g == place).astype(jnp.bfloat16)
        kept = jnp.dot(mask, spread, preferred_element_type=jnp.float32)
        selects.append(jnp.where(col == source, kept, 0.0).astype(jnp.bfloat16))
    for copy in copies:
        copy.wait()
    for k in range(len(targets)):
        for g, select in enumerate(selects):
            x = taken[k, g * rows : (g + 1) * rows, :]
            y = jnp.dot(select, x, preferred_element_type=jnp.float32).astype(jnp.bfloat16)
            for p in range(parts):
                for c in range(cols):
                    at = (p * cols + c) * per
                    out_refs[k][p, g * per : (g + 1) * per, c * LANES : (c + 1) * LANES] = y[at : at + per]


def join_kernel(order, me_ref, *refs):
    v_ref = refs[-1]
    size = refs[0].shape[1]
    for d, block_ref in zip(order, refs[:-1]):
        start = pl.multiple_of(lax.bitwise_xor(me_ref[0], d) * size, size)
        v_ref[:, pl.ds(start, size), :] = block_ref[...]


def corner_turn(volt, mask, table):
    parts = lax.axis_size("inp")
    _, size, both, frames = volt.shape
    me = lax.axis_index("inp").reshape(1)
    cols = frames // LANES
    chunk = size * cols * both
    rows = volt.reshape(parts, size, both, cols, LANES).transpose(0, 1, 3, 2, 4).reshape(parts * chunk, LANES)
    far = list(range(parts // 2, parts))
    near = sorted(range(1, parts // 2), key=lambda d: (-d.bit_length(), d))
    order = far[:1]
    for d, other in zip(near, far[1:]):
        order += [other, d]
    order.append(0)
    shape = (both, size, frames)
    blocks = []
    cuts = [0, *range(FIRST, GROUP, FIRST), *range(GROUP, parts, GROUP), parts]
    groups = [order[start:stop] for start, stop in zip(cuts, cuts[1:])][::-1]
    for targets in groups:
        extra = [in_hbm(table)] if 0 in targets else []
        fronts = pl.pallas_call(
            functools.partial(front_kernel, targets, min(size, 16)),
            out_shape=[small(parts)(shape, volt.dtype)] * len(targets)
            + [pltpu.VMEM(x.shape, x.dtype) for x in extra],
            in_specs=[SMEM, HBM, HBM] + [HBM] * len(extra),
            out_specs=[VMEM] * (len(targets) + len(extra)),
            scratch_shapes=[
                pltpu.VMEM((len(targets), chunk, LANES), volt.dtype),
                pltpu.VMEM((1, size), mask.dtype),
                pltpu.SemaphoreType.DMA((len(targets) + 2,)),
            ],
            compiler_params=pltpu.CompilerParams(vmem_limit_bytes=8 << 20),
            name="front",
        )(me, in_hbm(mask.reshape(1, size)), in_hbm(rows), *extra)
        if 0 in targets:
            staged_table = fronts[-1]
        for d, block in zip(targets, fronts):
            pairs = [(j, j ^ d) for j in range(parts)]
            blocks.append(lax.ppermute(block, "inp", pairs) if d else block)
    joined = pl.pallas_call(
        functools.partial(join_kernel, sum(groups, [])),
        out_shape=pltpu.VMEM((both, parts * size, frames), volt.dtype),
        in_specs=[SMEM] + [VMEM] * parts,
        out_specs=VMEM,
        compiler_params=pltpu.CompilerParams(vmem_limit_bytes=4 << 20),
        name="join",
    )(me, *[in_vmem(block, parts // 8) for block in blocks])
    return joined, staged_table


def in_hbm(x):
    return pltpu.with_memory_space_constraint(x, pltpu.HBM)


def small(parts):
    return pltpu.VMEM if parts <= 16 else jax.ShapeDtypeStruct


def sent_kernel(owners, slots, table_ref, me_ref, v_ref, *out_refs):
    for d in range(1, owners):
        owner = lax.rem(me_ref[0] + d, owners)
        for s in range(RAW):
            both = product(v_ref, table_ref[owner * slots + s])
            out_refs[d - 1][s, 0] = both[:TB]
            out_refs[d - 1][s, 1] = both[TB:]


def own_kernel(slots, table_ref, me_ref, v_ref, gains_ref, vis_ref, held, sem):
    me = me_ref[0]
    for s in range(KPO):
        tile = table_ref[me * slots + s]
        both = product(v_ref, tile)
        scale = outer(gains_ref, tile)
        held[s, 0] = (scale * both[:TB]).astype(jnp.bfloat16)
        held[s, 1] = (scale * both[TB:]).astype(jnp.bfloat16)
    copy = pltpu.make_async_copy(held, vis_ref.at[me], sem)
    copy.start()
    copy.wait()


def others_kernel(owners, slots, table_ref, me_ref, *refs):
    away = owners - 1
    tile_refs, ready_refs, gain_refs = refs[:away], refs[away : 2 * away], refs[2 * away : 3 * away]
    vis_ref, held, sem = refs[-3:]
    me = me_ref[0]
    copies = []
    for d in range(1, owners):
        to = vis_ref.at[lax.rem(me + owners - d, owners)]
        copies.append(pltpu.make_async_copy(ready_refs[d - 1], to.at[pl.ds(RAW, KPO - RAW)], sem.at[d - 1, RAW]))
        copies[-1].start()
        for s in range(RAW):
            scale = outer(gain_refs[d - 1], table_ref[me * slots + s])
            for part in range(2):
                held[d - 1, s, part] = (scale * tile_refs[d - 1][s, part]).astype(jnp.bfloat16)
            copies.append(pltpu.make_async_copy(held.at[d - 1, s], to.at[s], sem.at[d - 1, s]))
            copies[-1].start()
    for copy in copies:
        copy.wait()


def in_vmem(x, owners=2):
    return x if owners > 2 else pltpu.with_memory_space_constraint(x, pltpu.VMEM)


def body(volt, mask, table):
    owners = lax.axis_size("chan")
    slots = table.shape[0] // owners
    flat, table = (in_vmem(x) for x in corner_turn(volt, mask, table))
    _, count, frames = flat.shape
    me = lax.axis_index("chan").reshape(1)
    blocks = count // TB

    def shift(x, d):
        return lax.ppermute(x, "chan", [(j, (j + d) % owners) for j in range(owners)])

    sent = pl.pallas_call(
        functools.partial(sent_kernel, owners, slots),
        out_shape=[(pltpu.VMEM if owners == 2 else jax.ShapeDtypeStruct)((RAW, 2, TB, TB), jnp.float32)] * (owners - 1),
        in_specs=[SMEM, SMEM, VMEM],
        out_specs=[VMEM] * (owners - 1),
        compiler_params=pltpu.CompilerParams(vmem_limit_bytes=12 << 20),
        name="sent",
    )(table, me, flat)
    arrived = [in_vmem(shift(sent[d - 1], d), owners) for d in range(1, owners)]

    gains, by_block, *ready = pl.pallas_call(
        functools.partial(calibrate_kernel, owners, slots),
        out_shape=[
            jax.ShapeDtypeStruct((1, count), jnp.float32),
            pltpu.VMEM((blocks, TB), jnp.float32),
        ]
        + [small(8 * owners)((KPO - RAW, 2, TB, TB), jnp.bfloat16)] * (owners - 1),
        in_specs=[SMEM, SMEM, VMEM, VMEM],
        out_specs=[VMEM] * (owners + 1),
        scratch_shapes=[pltpu.VMEM((2, frames, count), jnp.bfloat16)],
        compiler_params=pltpu.CompilerParams(vmem_limit_bytes=12 << 20),
        name="calibrate",
    )(table, me, flat, in_vmem(jnp.asarray(first_basis(count))))
    other_gains = [in_vmem(shift(by_block, d), owners) for d in range(1, owners)]
    ready = [in_vmem(shift(ready[d - 1], d), owners) for d in range(1, owners)]

    vis_shape = jax.ShapeDtypeStruct((owners, KPO, 2, TB, TB), jnp.bfloat16)
    vis = pl.pallas_call(
        functools.partial(own_kernel, slots),
        out_shape=vis_shape,
        in_specs=[SMEM, SMEM, VMEM, VMEM],
        out_specs=ANY,
        scratch_shapes=[pltpu.VMEM((KPO, 2, TB, TB), jnp.bfloat16), pltpu.SemaphoreType.DMA],
        compiler_params=pltpu.CompilerParams(vmem_limit_bytes=12 << 20),
        name="own",
    )(table, me, flat, by_block)
    vis = pl.pallas_call(
        functools.partial(others_kernel, owners, slots),
        out_shape=vis_shape,
        in_specs=[SMEM, SMEM] + [VMEM] * (3 * owners - 3) + [ANY],
        out_specs=ANY,
        scratch_shapes=[
            pltpu.VMEM((owners - 1, RAW, 2, TB, TB), jnp.bfloat16),
            pltpu.SemaphoreType.DMA((owners - 1, RAW + 1)),
        ],
        input_output_aliases={3 * owners - 1: 0},
        compiler_params=pltpu.CompilerParams(vmem_limit_bytes=12 << 20),
        name="others",
    )(table, me, *arrived, *ready, *other_gains, vis)
    return (vis[None, :, None], gains.reshape(1, 1, count))


def solution(mesh):
    placed = (P("chan", "inp", None, None), P("inp"), P())
    return jax.shard_map(
        body,
        mesh=mesh,
        in_specs=placed,
        out_specs=(P("inp", None, "chan", None, None, None, None), P("chan", "inp", None)),
        check_vma=False,
    )
```

```python
import functools
import math

import jax
import jax.numpy as jnp
import numpy as np
from jax import lax
from jax.experimental import pallas as pl
from jax.experimental.pallas import tpu as pltpu
from jax.sharding import PartitionSpec as P

TB = 128
RANK = 4
ITERS = 8
KPO = 4
EPS = 1e-06
LANES = 128
GROUP = 4
FIRST = 2
RAW = 3
TERMS = 2
FIRST_TERMS = 3

VMEM = pl.BlockSpec(memory_space=pltpu.VMEM)
ANY = pl.BlockSpec(memory_space=pl.ANY)
HBM = pl.BlockSpec(memory_space=pltpu.HBM)
SMEM = pl.BlockSpec(memory_space=pltpu.SMEM)


def first_basis(count):
    turns = np.outer(np.arange(RANK), np.arange(count)) % count
    angle = 2.0 * math.pi / count * turns
    both = np.concatenate([np.cos(angle), np.sin(angle)], axis=0)
    return (both / math.sqrt(count)).astype(np.float32)


def pieces(x, terms):
    parts = []
    rest = x
    for k in range(terms):
        part = rest.astype(jnp.bfloat16).astype(jnp.float32)
        parts.append(part)
        rest = rest - part
    return jnp.concatenate(parts, axis=0).astype(jnp.bfloat16)


def dot(x, y):
    split = lax.dot_general(x, y, (((1,), (0,)), ((), ())), preferred_element_type=jnp.float32)
    rows = 2 * RANK
    last = split.shape[0] - rows
    total = split[last:]
    for k in range(last - rows, -1, -rows):
        total = total + split[k : k + rows]
    return total


def swap(x):
    return jnp.concatenate([x[RANK:], x[:RANK]], axis=0)


def inner(row_real, row_imag, z, turned):
    first = jnp.sum(z * row_real + turned * row_imag, axis=1, keepdims=True)
    second = jnp.sum(z * row_imag - turned * row_real, axis=1, keepdims=True)
    return first, second


def times(x, k, first, second):
    return x[k : k + 1] * first + x[RANK + k : RANK + k + 1] * second


def gram_schmidt(z, p, sign, order):
    turned = sign * swap(z)
    w = z
    scales = jnp.zeros((2 * RANK, 1), jnp.float32)
    for l in range(RANK):
        row_real = w[l : l + 1]
        row_imag = w[RANK + l : RANK + l + 1]
        norm = jnp.sum(row_real * row_real + row_imag * row_imag, axis=1, keepdims=True)
        scale = lax.rsqrt(norm + EPS)
        scales = jnp.where(order == l, scale, scales)
        if l < RANK - 1:
            first, second = inner(row_real, row_imag, z, turned)
            keep = jnp.where(order > l, scale * scale, 0.0)
            first, second = first * keep, second * keep
            w = w - times(w, l, first, second)
            p = p - times(p, l, first, second)
    return w * scales, p * scales


def calibrate_kernel(owners, slots, table_ref, me_ref, v_ref, first, gains_ref, blocks_ref, *refs):
    ready_refs, vt_ref = refs[:-1], refs[-1]
    _, count, frames = v_ref.shape
    rows = lax.broadcasted_iota(jnp.int32, (2 * RANK, 1), 0)
    sign = jnp.where(rows < RANK, 1.0, -1.0)
    order = jnp.where(rows < RANK, rows, rows - RANK)
    for part in range(2):
        for k in range(0, count, 2 * TB):
            vt_ref[part, :, k : k + 2 * TB] = jnp.transpose(v_ref[part, k : k + 2 * TB, :])

    def project(q, terms=TERMS):
        x = pieces(q, terms)
        return dot(x, v_ref[0]) + sign * swap(dot(x, v_ref[1]))

    def expand(y, terms=TERMS):
        z = dot(pieces(y, terms), vt_ref[0]) - dot(pieces(sign * swap(y), terms), vt_ref[1])
        return z * (1.0 / frames)

    def step(_, z):
        return expand(gram_schmidt(z, project(z), sign, order)[1])

    z = expand(project(first[...], FIRST_TERMS), FIRST_TERMS)
    z = expand(gram_schmidt(z, project(z, FIRST_TERMS), sign, order)[1])
    z = lax.fori_loop(0, ITERS - 2, step, z)
    q, y = gram_schmidt(z, project(z), sign, order)
    turned = sign * swap(y)
    u = jnp.zeros_like(q)
    for k in range(RANK):
        u = u + times(q, k, *inner(y[k : k + 1], y[RANK + k : RANK + k + 1], y, turned))
    d = jnp.sum(u * q, axis=0, keepdims=True) * (1.0 / frames)
    floor = 0.1 * (jnp.sum(d, axis=1, keepdims=True) / count) + EPS
    gains = lax.rsqrt(jnp.maximum(d, floor))
    gains_ref[...] = gains
    for k in range(count // TB):
        blocks_ref[k : k + 1, :] = gains[:, k * TB : (k + 1) * TB]
    for d in range(1, owners):
        owner = lax.rem(me_ref[0] + d, owners)
        for s in range(RAW, KPO):
            tile = table_ref[owner * slots + s]
            both = product(v_ref, tile)
            scale = outer(blocks_ref, tile)
            ready_refs[d - 1][s - RAW, 0] = (scale * both[:TB]).astype(jnp.bfloat16)
            ready_refs[d - 1][s - RAW, 1] = (scale * both[TB:]).astype(jnp.bfloat16)


def product(v_ref, tile):
    _, count, frames = v_ref.shape
    blocks = count // TB
    row = pl.ds(pl.multiple_of((tile // blocks) * TB, TB), TB)
    col = pl.ds(pl.multiple_of(lax.rem(tile, blocks) * TB, TB), TB)
    real, imag, col_real, col_imag = (v_ref[part, k, :] for k in (row, col) for part in range(2))
    dims = (((1,), (1,)), ((), ()))
    both = lax.dot_general(
        jnp.concatenate([real, imag], axis=0), col_real, dims, preferred_element_type=jnp.float32
    )
    both = both + lax.dot_general(
        jnp.concatenate([imag, -real], axis=0), col_imag, dims, preferred_element_type=jnp.float32
    )
    return both * (1.0 / frames)


def outer(gains_ref, tile):
    blocks = gains_ref.shape[0]
    row = gains_ref[pl.ds(tile // blocks, 1), :]
    col = gains_ref[pl.ds(lax.rem(tile, blocks), 1), :]
    return jnp.transpose(jnp.broadcast_to(row, (TB, TB))) * col


def front_kernel(targets, per, me_ref, mask_ref, volt_ref, *refs):
    if 0 in targets:
        table_ref, *refs = refs
        staged_ref = refs.pop(len(targets))
    out_refs, (taken, flags, sem) = refs[: len(targets)], refs[len(targets) :]
    parts, size, frames = out_refs[0].shape
    cols = frames // LANES
    rows = per * cols * parts
    chunk = taken.shape[1]
    copies = []
    for k, d in enumerate(targets):
        start = pl.multiple_of(lax.bitwise_xor(me_ref[0], d) * chunk, chunk)
        copies.append(pltpu.make_async_copy(volt_ref.at[pl.ds(start, chunk)], taken.at[k], sem.at[k]))
        copies[-1].start()
    flag_copy = pltpu.make_async_copy(mask_ref, flags, sem.at[len(targets)])
    flag_copy.start()
    if 0 in targets:
        copies.append(pltpu.make_async_copy(table_ref, staged_ref, sem.at[len(targets) + 1]))
        copies[-1].start()
    row = lax.broadcasted_iota(jnp.int32, (rows, rows), 0)
    col = lax.broadcasted_iota(jnp.int32, (rows, rows), 1)
    block = lax.div(row, per)
    source = (lax.rem(row, per) * cols + lax.rem(block, cols)) * parts + lax.div(block, cols)
    lane = lax.broadcasted_iota(jnp.int32, (size, rows), 1)
    place = lax.broadcasted_iota(jnp.int32, (size, rows), 0)
    flag_copy.wait()
    mask = flags[...].astype(jnp.bfloat16)
    selects = []
    for g in range(0, size, per):
        spread = (lax.div(lane, cols * parts) + g == place).astype(jnp.bfloat16)
        kept = jnp.dot(mask, spread, preferred_element_type=jnp.float32)
        selects.append(jnp.where(col == source, kept, 0.0).astype(jnp.bfloat16))
    for copy in copies:
        copy.wait()
    for k in range(len(targets)):
        for g, select in enumerate(selects):
            x = taken[k, g * rows : (g + 1) * rows, :]
            y = jnp.dot(select, x, preferred_element_type=jnp.float32).astype(jnp.bfloat16)
            for p in range(parts):
                for c in range(cols):
                    at = (p * cols + c) * per
                    out_refs[k][p, g * per : (g + 1) * per, c * LANES : (c + 1) * LANES] = y[at : at + per]


def join_kernel(order, me_ref, *refs):
    v_ref = refs[-1]
    size = refs[0].shape[1]
    for d, block_ref in zip(order, refs[:-1]):
        start = pl.multiple_of(lax.bitwise_xor(me_ref[0], d) * size, size)
        v_ref[:, pl.ds(start, size), :] = block_ref[...]


def corner_turn(volt, mask, table):
    parts = lax.axis_size("inp")
    _, size, both, frames = volt.shape
    me = lax.axis_index("inp").reshape(1)
    cols = frames // LANES
    chunk = size * cols * both
    rows = volt.reshape(parts, size, both, cols, LANES).transpose(0, 1, 3, 2, 4).reshape(parts * chunk, LANES)
    far = list(range(parts // 2, parts))
    near = sorted(range(1, parts // 2), key=lambda d: (-d.bit_length(), d))
    order = far[:1]
    for d, other in zip(near, far[1:]):
        order += [other, d]
    order.append(0)
    shape = (both, size, frames)
    blocks = []
    cuts = [0, *range(FIRST, GROUP, FIRST), *range(GROUP, parts, GROUP), parts]
    groups = [order[start:stop] for start, stop in zip(cuts, cuts[1:])][::-1]
    for targets in groups:
        extra = [in_hbm(table)] if 0 in targets else []
        fronts = pl.pallas_call(
            functools.partial(front_kernel, targets, min(size, 16)),
            out_shape=[small(parts)(shape, volt.dtype)] * len(targets)
            + [pltpu.VMEM(x.shape, x.dtype) for x in extra],
            in_specs=[SMEM, HBM, HBM] + [HBM] * len(extra),
            out_specs=[VMEM] * (len(targets) + len(extra)),
            scratch_shapes=[
                pltpu.VMEM((len(targets), chunk, LANES), volt.dtype),
                pltpu.VMEM((1, size), mask.dtype),
                pltpu.SemaphoreType.DMA((len(targets) + 2,)),
            ],
            compiler_params=pltpu.CompilerParams(vmem_limit_bytes=8 << 20),
            name="front",
        )(me, in_hbm(mask.reshape(1, size)), in_hbm(rows), *extra)
        if 0 in targets:
            staged_table = fronts[-1]
        for d, block in zip(targets, fronts):
            pairs = [(j, j ^ d) for j in range(parts)]
            blocks.append(lax.ppermute(block, "inp", pairs) if d else block)
    joined = pl.pallas_call(
        functools.partial(join_kernel, sum(groups, [])),
        out_shape=pltpu.VMEM((both, parts * size, frames), volt.dtype),
        in_specs=[SMEM] + [VMEM] * parts,
        out_specs=VMEM,
        compiler_params=pltpu.CompilerParams(vmem_limit_bytes=4 << 20),
        name="join",
    )(me, *[in_vmem(block, parts // 8) for block in blocks])
    return joined, staged_table


def in_hbm(x):
    return pltpu.with_memory_space_constraint(x, pltpu.HBM)


def small(parts):
    return pltpu.VMEM if parts <= 16 else jax.ShapeDtypeStruct


def sent_kernel(owners, slots, table_ref, me_ref, v_ref, *out_refs):
    for d in range(1, owners):
        owner = lax.rem(me_ref[0] + d, owners)
        for s in range(RAW):
            both = product(v_ref, table_ref[owner * slots + s])
            out_refs[d - 1][s, 0] = both[:TB]
            out_refs[d - 1][s, 1] = both[TB:]


def own_kernel(slots, table_ref, me_ref, v_ref, gains_ref, vis_ref, held, sem):
    me = me_ref[0]
    for s in range(KPO):
        tile = table_ref[me * slots + s]
        both = product(v_ref, tile)
        scale = outer(gains_ref, tile)
        held[s, 0] = (scale * both[:TB]).astype(jnp.bfloat16)
        held[s, 1] = (scale * both[TB:]).astype(jnp.bfloat16)
    copy = pltpu.make_async_copy(held, vis_ref.at[me], sem)
    copy.start()
    copy.wait()


def others_kernel(owners, slots, table_ref, me_ref, *refs):
    away = owners - 1
    tile_refs, ready_refs, gain_refs = refs[:away], refs[away : 2 * away], refs[2 * away : 3 * away]
    vis_ref, held, sem = refs[-3:]
    me = me_ref[0]
    copies = []
    for d in range(1, owners):
        to = vis_ref.at[lax.rem(me + owners - d, owners)]
        copies.append(pltpu.make_async_copy(ready_refs[d - 1], to.at[pl.ds(RAW, KPO - RAW)], sem.at[d - 1, RAW]))
        copies[-1].start()
        for s in range(RAW):
            scale = outer(gain_refs[d - 1], table_ref[me * slots + s])
            for part in range(2):
                held[d - 1, s, part] = (scale * tile_refs[d - 1][s, part]).astype(jnp.bfloat16)
            copies.append(pltpu.make_async_copy(held.at[d - 1, s], to.at[s], sem.at[d - 1, s]))
            copies[-1].start()
    for copy in copies:
        copy.wait()


def in_vmem(x, owners=2):
    return x if owners > 2 else pltpu.with_memory_space_constraint(x, pltpu.VMEM)


def body(volt, mask, table):
    owners = lax.axis_size("chan")
    slots = table.shape[0] // owners
    flat, table = (in_vmem(x) for x in corner_turn(volt, mask, table))
    _, count, frames = flat.shape
    me = lax.axis_index("chan").reshape(1)
    blocks = count // TB

    def shift(x, d):
        return lax.ppermute(x, "chan", [(j, (j + d) % owners) for j in range(owners)])

    sent = pl.pallas_call(
        functools.partial(sent_kernel, owners, slots),
        out_shape=[(pltpu.VMEM if owners == 2 else jax.ShapeDtypeStruct)((RAW, 2, TB, TB), jnp.float32)] * (owners - 1),
        in_specs=[SMEM, SMEM, VMEM],
        out_specs=[VMEM] * (owners - 1),
        compiler_params=pltpu.CompilerParams(vmem_limit_bytes=12 << 20),
        name="sent",
    )(table, me, flat)
    arrived = [in_vmem(shift(sent[d - 1], d), owners) for d in range(1, owners)]

    gains, by_block, *ready = pl.pallas_call(
        functools.partial(calibrate_kernel, owners, slots),
        out_shape=[
            jax.ShapeDtypeStruct((1, count), jnp.float32),
            pltpu.VMEM((blocks, TB), jnp.float32),
        ]
        + [small(8 * owners)((KPO - RAW, 2, TB, TB), jnp.bfloat16)] * (owners - 1),
        in_specs=[SMEM, SMEM, VMEM, VMEM],
        out_specs=[VMEM] * (owners + 1),
        scratch_shapes=[pltpu.VMEM((2, frames, count), jnp.bfloat16)],
        compiler_params=pltpu.CompilerParams(vmem_limit_bytes=12 << 20),
        name="calibrate",
    )(table, me, flat, in_vmem(jnp.asarray(first_basis(count))))
    other_gains = [in_vmem(shift(by_block, d), owners) for d in range(1, owners)]
    ready = [in_vmem(shift(ready[d - 1], d), owners) for d in range(1, owners)]

    vis_shape = jax.ShapeDtypeStruct((owners, KPO, 2, TB, TB), jnp.bfloat16)
    vis = pl.pallas_call(
        functools.partial(own_kernel, slots),
        out_shape=vis_shape,
        in_specs=[SMEM, SMEM, VMEM, VMEM],
        out_specs=ANY,
        scratch_shapes=[pltpu.VMEM((KPO, 2, TB, TB), jnp.bfloat16), pltpu.SemaphoreType.DMA],
        compiler_params=pltpu.CompilerParams(vmem_limit_bytes=12 << 20),
        name="own",
    )(table, me, flat, by_block)
    vis = pl.pallas_call(
        functools.partial(others_kernel, owners, slots),
        out_shape=vis_shape,
        in_specs=[SMEM, SMEM] + [VMEM] * (3 * owners - 3) + [ANY],
        out_specs=ANY,
        scratch_shapes=[
            pltpu.VMEM((owners - 1, RAW, 2, TB, TB), jnp.bfloat16),
            pltpu.SemaphoreType.DMA((owners - 1, RAW + 1)),
        ],
        input_output_aliases={3 * owners - 1: 0},
        compiler_params=pltpu.CompilerParams(vmem_limit_bytes=12 << 20),
        name="others",
    )(table, me, *arrived, *ready, *other_gains, vis)
    return (vis[None, :, None], gains.reshape(1, 1, count))


def solution(mesh):
    placed = (P("chan", "inp", None, None), P("inp"), P())
    return jax.shard_map(
        body,
        mesh=mesh,
        in_specs=placed,
        out_specs=(P("inp", None, "chan", None, None, None, None), P("chan", "inp", None)),
        check_vma=False,
    )
```

```python
import functools
import math

import jax
import jax.numpy as jnp
import numpy as np
from jax import lax
from jax.experimental import pallas as pl
from jax.experimental.pallas import tpu as pltpu
from jax.sharding import PartitionSpec as P

TB = 128
RANK = 4
ITERS = 8
KPO = 4
EPS = 1e-06
LANES = 128
GROUP = 4
FIRST = 2
RAW = 3
TERMS = 2
FIRST_TERMS = 3

VMEM = pl.BlockSpec(memory_space=pltpu.VMEM)
ANY = pl.BlockSpec(memory_space=pl.ANY)
HBM = pl.BlockSpec(memory_space=pltpu.HBM)
SMEM = pl.BlockSpec(memory_space=pltpu.SMEM)


def first_basis(count):
    turns = np.outer(np.arange(RANK), np.arange(count)) % count
    angle = 2.0 * math.pi / count * turns
    both = np.concatenate([np.cos(angle), np.sin(angle)], axis=0)
    return (both / math.sqrt(count)).astype(np.float32)


def pieces(x, terms):
    parts = []
    rest = x
    for k in range(terms):
        part = rest.astype(jnp.bfloat16).astype(jnp.float32)
        parts.append(part)
        rest = rest - part
    return jnp.concatenate(parts, axis=0).astype(jnp.bfloat16)


def dot(x, y):
    split = lax.dot_general(x, y, (((1,), (0,)), ((), ())), preferred_element_type=jnp.float32)
    rows = 2 * RANK
    last = split.shape[0] - rows
    total = split[last:]
    for k in range(last - rows, -1, -rows):
        total = total + split[k : k + rows]
    return total


def swap(x):
    return jnp.concatenate([x[RANK:], x[:RANK]], axis=0)


def inner(row_real, row_imag, z, turned):
    first = jnp.sum(z * row_real + turned * row_imag, axis=1, keepdims=True)
    second = jnp.sum(z * row_imag - turned * row_real, axis=1, keepdims=True)
    return first, second


def times(x, k, first, second):
    return x[k : k + 1] * first + x[RANK + k : RANK + k + 1] * second


def gram_schmidt(z, p, sign, order):
    turned = sign * swap(z)
    w = z
    scales = jnp.zeros((2 * RANK, 1), jnp.float32)
    for l in range(RANK):
        row_real = w[l : l + 1]
        row_imag = w[RANK + l : RANK + l + 1]
        norm = jnp.sum(row_real * row_real + row_imag * row_imag, axis=1, keepdims=True)
        scale = lax.rsqrt(norm + EPS)
        scales = jnp.where(order == l, scale, scales)
        if l < RANK - 1:
            first, second = inner(row_real, row_imag, z, turned)
            keep = jnp.where(order > l, scale * scale, 0.0)
            first, second = first * keep, second * keep
            w = w - times(w, l, first, second)
            p = p - times(p, l, first, second)
    return w * scales, p * scales


def calibrate_kernel(owners, slots, table_ref, me_ref, v_ref, first, gains_ref, blocks_ref, *refs):
    ready_refs, vt_ref = refs[:-1], refs[-1]
    _, count, frames = v_ref.shape
    rows = lax.broadcasted_iota(jnp.int32, (2 * RANK, 1), 0)
    sign = jnp.where(rows < RANK, 1.0, -1.0)
    order = jnp.where(rows < RANK, rows, rows - RANK)
    for part in range(2):
        for k in range(0, count, 2 * TB):
            vt_ref[part, :, k : k + 2 * TB] = jnp.transpose(v_ref[part, k : k + 2 * TB, :])

    def project(q, terms=TERMS):
        x = pieces(q, terms)
        return dot(x, v_ref[0]) + sign * swap(dot(x, v_ref[1]))

    def expand(y, terms=TERMS):
        z = dot(pieces(y, terms), vt_ref[0]) - dot(pieces(sign * swap(y), terms), vt_ref[1])
        return z * (1.0 / frames)

    def step(_, z):
        return expand(gram_schmidt(z, project(z), sign, order)[1])

    z = expand(project(first[...], FIRST_TERMS), FIRST_TERMS)
    z = expand(project(gram_schmidt(z, z, sign, order)[0]))
    z = lax.fori_loop(0, ITERS - 2, step, z)
    q, y = gram_schmidt(z, project(z), sign, order)
    turned = sign * swap(y)
    u = jnp.zeros_like(q)
    for k in range(RANK):
        u = u + times(q, k, *inner(y[k : k + 1], y[RANK + k : RANK + k + 1], y, turned))
    d = jnp.sum(u * q, axis=0, keepdims=True) * (1.0 / frames)
    floor = 0.1 * (jnp.sum(d, axis=1, keepdims=True) / count) + EPS
    gains = lax.rsqrt(jnp.maximum(d, floor))
    gains_ref[...] = gains
    for k in range(count // TB):
        blocks_ref[k : k + 1, :] = gains[:, k * TB : (k + 1) * TB]
    for d in range(1, owners):
        owner = lax.rem(me_ref[0] + d, owners)
        for s in range(RAW, KPO):
            tile = table_ref[owner * slots + s]
            both = product(v_ref, tile)
            scale = outer(blocks_ref, tile)
            ready_refs[d - 1][s - RAW, 0] = (scale * both[:TB]).astype(jnp.bfloat16)
            ready_refs[d - 1][s - RAW, 1] = (scale * both[TB:]).astype(jnp.bfloat16)


def product(v_ref, tile):
    _, count, frames = v_ref.shape
    blocks = count // TB
    row = pl.ds(pl.multiple_of((tile // blocks) * TB, TB), TB)
    col = pl.ds(pl.multiple_of(lax.rem(tile, blocks) * TB, TB), TB)
    real, imag, col_real, col_imag = (v_ref[part, k, :] for k in (row, col) for part in range(2))
    dims = (((1,), (1,)), ((), ()))
    both = lax.dot_general(
        jnp.concatenate([real, imag], axis=0), col_real, dims, preferred_element_type=jnp.float32
    )
    both = both + lax.dot_general(
        jnp.concatenate([imag, -real], axis=0), col_imag, dims, preferred_element_type=jnp.float32
    )
    return both * (1.0 / frames)


def outer(gains_ref, tile):
    blocks = gains_ref.shape[0]
    row = gains_ref[pl.ds(tile // blocks, 1), :]
    col = gains_ref[pl.ds(lax.rem(tile, blocks), 1), :]
    return jnp.transpose(jnp.broadcast_to(row, (TB, TB))) * col


def front_kernel(targets, per, me_ref, mask_ref, volt_ref, *refs):
    if 0 in targets:
        table_ref, *refs = refs
        staged_ref = refs.pop(len(targets))
    out_refs, (taken, flags, sem) = refs[: len(targets)], refs[len(targets) :]
    parts, size, frames = out_refs[0].shape
    cols = frames // LANES
    rows = per * cols * parts
    chunk = taken.shape[1]
    copies = []
    for k, d in enumerate(targets):
        start = pl.multiple_of(lax.bitwise_xor(me_ref[0], d) * chunk, chunk)
        copies.append(pltpu.make_async_copy(volt_ref.at[pl.ds(start, chunk)], taken.at[k], sem.at[k]))
        copies[-1].start()
    flag_copy = pltpu.make_async_copy(mask_ref, flags, sem.at[len(targets)])
    flag_copy.start()
    if 0 in targets:
        copies.append(pltpu.make_async_copy(table_ref, staged_ref, sem.at[len(targets) + 1]))
        copies[-1].start()
    row = lax.broadcasted_iota(jnp.int32, (rows, rows), 0)
    col = lax.broadcasted_iota(jnp.int32, (rows, rows), 1)
    block = lax.div(row, per)
    source = (lax.rem(row, per) * cols + lax.rem(block, cols)) * parts + lax.div(block, cols)
    lane = lax.broadcasted_iota(jnp.int32, (size, rows), 1)
    place = lax.broadcasted_iota(jnp.int32, (size, rows), 0)
    flag_copy.wait()
    mask = flags[...].astype(jnp.bfloat16)
    selects = []
    for g in range(0, size, per):
        spread = (lax.div(lane, cols * parts) + g == place).astype(jnp.bfloat16)
        kept = jnp.dot(mask, spread, preferred_element_type=jnp.float32)
        selects.append(jnp.where(col == source, kept, 0.0).astype(jnp.bfloat16))
    for copy in copies:
        copy.wait()
    for k in range(len(targets)):
        for g, select in enumerate(selects):
            x = taken[k, g * rows : (g + 1) * rows, :]
            y = jnp.dot(select, x, preferred_element_type=jnp.float32).astype(jnp.bfloat16)
            for p in range(parts):
                for c in range(cols):
                    at = (p * cols + c) * per
                    out_refs[k][p, g * per : (g + 1) * per, c * LANES : (c + 1) * LANES] = y[at : at + per]


def join_kernel(order, me_ref, *refs):
    v_ref = refs[-1]
    size = refs[0].shape[1]
    for d, block_ref in zip(order, refs[:-1]):
        start = pl.multiple_of(lax.bitwise_xor(me_ref[0], d) * size, size)
        v_ref[:, pl.ds(start, size), :] = block_ref[...]


def corner_turn(volt, mask, table):
    parts = lax.axis_size("inp")
    _, size, both, frames = volt.shape
    me = lax.axis_index("inp").reshape(1)
    cols = frames // LANES
    chunk = size * cols * both
    rows = volt.reshape(parts, size, both, cols, LANES).transpose(0, 1, 3, 2, 4).reshape(parts * chunk, LANES)
    far = list(range(parts // 2, parts))
    near = sorted(range(1, parts // 2), key=lambda d: (-d.bit_length(), d))
    order = far[:1]
    for d, other in zip(near, far[1:]):
        order += [other, d]
    order.append(0)
    shape = (both, size, frames)
    blocks = []
    cuts = [0, *range(FIRST, GROUP, FIRST), *range(GROUP, parts, GROUP), parts]
    groups = [order[start:stop] for start, stop in zip(cuts, cuts[1:])][::-1]
    for targets in groups:
        extra = [in_hbm(table)] if 0 in targets else []
        fronts = pl.pallas_call(
            functools.partial(front_kernel, targets, min(size, 16)),
            out_shape=[small(parts)(shape, volt.dtype)] * len(targets)
            + [pltpu.VMEM(x.shape, x.dtype) for x in extra],
            in_specs=[SMEM, HBM, HBM] + [HBM] * len(extra),
            out_specs=[VMEM] * (len(targets) + len(extra)),
            scratch_shapes=[
                pltpu.VMEM((len(targets), chunk, LANES), volt.dtype),
                pltpu.VMEM((1, size), mask.dtype),
                pltpu.SemaphoreType.DMA((len(targets) + 2,)),
            ],
            compiler_params=pltpu.CompilerParams(vmem_limit_bytes=8 << 20),
            name="front",
        )(me, in_hbm(mask.reshape(1, size)), in_hbm(rows), *extra)
        if 0 in targets:
            staged_table = fronts[-1]
        for d, block in zip(targets, fronts):
            pairs = [(j, j ^ d) for j in range(parts)]
            blocks.append(lax.ppermute(block, "inp", pairs) if d else block)
    joined = pl.pallas_call(
        functools.partial(join_kernel, sum(groups, [])),
        out_shape=pltpu.VMEM((both, parts * size, frames), volt.dtype),
        in_specs=[SMEM] + [VMEM] * parts,
        out_specs=VMEM,
        compiler_params=pltpu.CompilerParams(vmem_limit_bytes=4 << 20),
        name="join",
    )(me, *[in_vmem(block, parts // 8) for block in blocks])
    return joined, staged_table


def in_hbm(x):
    return pltpu.with_memory_space_constraint(x, pltpu.HBM)


def small(parts):
    return pltpu.VMEM if parts <= 16 else jax.ShapeDtypeStruct


def sent_kernel(owners, slots, table_ref, me_ref, v_ref, *out_refs):
    for d in range(1, owners):
        owner = lax.rem(me_ref[0] + d, owners)
        for s in range(RAW):
            both = product(v_ref, table_ref[owner * slots + s])
            out_refs[d - 1][s, 0] = both[:TB]
            out_refs[d - 1][s, 1] = both[TB:]


def own_kernel(slots, table_ref, me_ref, v_ref, gains_ref, vis_ref, held, sem):
    me = me_ref[0]
    for s in range(KPO):
        tile = table_ref[me * slots + s]
        both = product(v_ref, tile)
        scale = outer(gains_ref, tile)
        held[s, 0] = (scale * both[:TB]).astype(jnp.bfloat16)
        held[s, 1] = (scale * both[TB:]).astype(jnp.bfloat16)
    copy = pltpu.make_async_copy(held, vis_ref.at[me], sem)
    copy.start()
    copy.wait()


def others_kernel(owners, slots, table_ref, me_ref, *refs):
    away = owners - 1
    tile_refs, ready_refs, gain_refs = refs[:away], refs[away : 2 * away], refs[2 * away : 3 * away]
    vis_ref, held, sem = refs[-3:]
    me = me_ref[0]
    copies = []
    for d in range(1, owners):
        to = vis_ref.at[lax.rem(me + owners - d, owners)]
        copies.append(pltpu.make_async_copy(ready_refs[d - 1], to.at[pl.ds(RAW, KPO - RAW)], sem.at[d - 1, RAW]))
        copies[-1].start()
        for s in range(RAW):
            scale = outer(gain_refs[d - 1], table_ref[me * slots + s])
            for part in range(2):
                held[d - 1, s, part] = (scale * tile_refs[d - 1][s, part]).astype(jnp.bfloat16)
            copies.append(pltpu.make_async_copy(held.at[d - 1, s], to.at[s], sem.at[d - 1, s]))
            copies[-1].start()
    for copy in copies:
        copy.wait()


def in_vmem(x, owners=2):
    return x if owners > 2 else pltpu.with_memory_space_constraint(x, pltpu.VMEM)


def body(volt, mask, table):
    owners = lax.axis_size("chan")
    slots = table.shape[0] // owners
    flat, table = (in_vmem(x) for x in corner_turn(volt, mask, table))
    _, count, frames = flat.shape
    me = lax.axis_index("chan").reshape(1)
    blocks = count // TB

    def shift(x, d):
        return lax.ppermute(x, "chan", [(j, (j + d) % owners) for j in range(owners)])

    sent = pl.pallas_call(
        functools.partial(sent_kernel, owners, slots),
        out_shape=[(pltpu.VMEM if owners == 2 else jax.ShapeDtypeStruct)((RAW, 2, TB, TB), jnp.float32)] * (owners - 1),
        in_specs=[SMEM, SMEM, VMEM],
        out_specs=[VMEM] * (owners - 1),
        compiler_params=pltpu.CompilerParams(vmem_limit_bytes=12 << 20),
        name="sent",
    )(table, me, flat)
    arrived = [in_vmem(shift(sent[d - 1], d), owners) for d in range(1, owners)]

    gains, by_block, *ready = pl.pallas_call(
        functools.partial(calibrate_kernel, owners, slots),
        out_shape=[
            jax.ShapeDtypeStruct((1, count), jnp.float32),
            pltpu.VMEM((blocks, TB), jnp.float32),
        ]
        + [small(8 * owners)((KPO - RAW, 2, TB, TB), jnp.bfloat16)] * (owners - 1),
        in_specs=[SMEM, SMEM, VMEM, VMEM],
        out_specs=[VMEM] * (owners + 1),
        scratch_shapes=[pltpu.VMEM((2, frames, count), jnp.bfloat16)],
        compiler_params=pltpu.CompilerParams(vmem_limit_bytes=12 << 20),
        name="calibrate",
    )(table, me, flat, in_vmem(jnp.asarray(first_basis(count))))
    other_gains = [in_vmem(shift(by_block, d), owners) for d in range(1, owners)]
    ready = [in_vmem(shift(ready[d - 1], d), owners) for d in range(1, owners)]

    vis_shape = jax.ShapeDtypeStruct((owners, KPO, 2, TB, TB), jnp.bfloat16)
    vis = pl.pallas_call(
        functools.partial(own_kernel, slots),
        out_shape=vis_shape,
        in_specs=[SMEM, SMEM, VMEM, VMEM],
        out_specs=ANY,
        scratch_shapes=[pltpu.VMEM((KPO, 2, TB, TB), jnp.bfloat16), pltpu.SemaphoreType.DMA],
        compiler_params=pltpu.CompilerParams(vmem_limit_bytes=12 << 20),
        name="own",
    )(table, me, flat, by_block)
    vis = pl.pallas_call(
        functools.partial(others_kernel, owners, slots),
        out_shape=vis_shape,
        in_specs=[SMEM, SMEM] + [VMEM] * (3 * owners - 3) + [ANY],
        out_specs=ANY,
        scratch_shapes=[
            pltpu.VMEM((owners - 1, RAW, 2, TB, TB), jnp.bfloat16),
            pltpu.SemaphoreType.DMA((owners - 1, RAW + 1)),
        ],
        input_output_aliases={3 * owners - 1: 0},
        compiler_params=pltpu.CompilerParams(vmem_limit_bytes=12 << 20),
        name="others",
    )(table, me, *arrived, *ready, *other_gains, vis)
    return (vis[None, :, None], gains.reshape(1, 1, count))


def solution(mesh):
    placed = (P("chan", "inp", None, None), P("inp"), P())
    return jax.shard_map(
        body,
        mesh=mesh,
        in_specs=placed,
        out_specs=(P("inp", None, "chan", None, None, None, None), P("chan", "inp", None)),
        check_vma=False,
    )
```
